768 devices in a mesh: batch: 8 (over y), row: 8 (over z_lo, core), col: 12 (over x, z_hi).
Axes of the slice: x: 4, y: 8, z: 12 (z_hi: 3, z_lo: 4; z = z_hi * 4 + z_lo), core: 2. Of those that a mesh axis runs over, the one named last changes fastest.
Arguments:
- tokens: bfloat16 [4096, 6144], P('batch', 'row'), may hold values from -6 to 6
- cotangent: bfloat16 [4096, 6144], P('batch', 'row'), may hold values from -1.5 to 1.5
- weight_in: bfloat16 [6144, 12288], P('row', 'col'), may hold values from -0.078125 to 0.078125
- weight_out: bfloat16 [12288, 6144], P('col', 'row'), may hold values from -0.0546875 to 0.0546875
- segment_ids: int32 [4096], P('batch'), may hold values from 0 to 31, as said below
- keep_mask: int32 [4096], P('batch'), may hold values 0 or 1
Outputs:
- grad_tokens: bfloat16 [4096, 6144], P('batch', 'row')
- grad_weight_in: bfloat16 [6144, 12288], P(('row', 'batch'), 'col')
- grad_weight_out: bfloat16 [12288, 6144], P('col', ('row', 'batch'))
The draws below stay inside these ranges and needn't reach their ends.
Inputs may be any that keep to these rules, and one draw needn't show every extreme that they name: `segment_ids`: never falling along the bin; every image 0 .. 31 has 1 to 192 tokens, and some image has exactly 192.
All inputs are finite; a program needn't handle non-finite values. No bound on the sum of `keep_mask` on one device may be relied on, other than what follows from the above.
Results may differ from the reference program's by a relative error of at most 0.023.
Values may be sent and summed in bfloat16 or wider, within the bound.
A program may use at most 32 MiB of HBM per device.

```python
import jax
import jax.numpy as jnp
from jax import lax

D = 6144
FF = 12288
TOKENS = 4096
SEGS = 32
IMAGE_MEAN = 128
N_BATCH = 8
N_ROW = 8
N_COL = 12


def draw_segment_ids(key, part):
    jitter_key = jax.random.fold_in(key, 17)
    count = SEGS - 1
    index = jnp.arange(count, dtype=jnp.int32)
    jitter_width = IMAGE_MEAN // 8
    jitter = jax.random.randint(jitter_key, (count,), -jitter_width, jitter_width + 1, dtype=jnp.int32)
    jitter = jnp.where(index == count - 1, 0, jitter)
    cuts = index * IMAGE_MEAN + IMAGE_MEAN // 2 + jitter
    places = jnp.arange(TOKENS, dtype=jnp.int32)
    return jnp.sum((places[:, None] >= cuts[None, :]).astype(jnp.int32), axis=1).astype(jnp.int32)


def set_ends(result, rng, smallest, high):
    shape = result.shape
    place = [jax.random.randint(jax.random.fold_in(rng, axis), (), 0, shape[axis]) for axis in range(len(shape))]
    result = result.at[tuple(place)].set(smallest)
    longest = shape.index(max(shape))
    place[longest] = (place[longest] + 1) % shape[longest]
    return result.at[tuple(place)].set(high)


def block_scale(key, dims, pieces, smallest, top_value):
    def one(axis_at, parts):
        steps = jax.random.uniform(jax.random.fold_in(jax.random.fold_in(key, 6), axis_at), (parts,), jnp.float32, smallest / len(pieces), top_value / len(pieces))
        return jnp.repeat(jnp.exp(steps), dims[axis_at] // parts).reshape((-1,) + (1,) * (len(dims) - axis_at - 1))

    factor_of = one(*pieces[0])
    for cut in pieces[1:]:
        factor_of = factor_of * one(*cut)
    return factor_of


def gaussian(rng, dims, deviation, bound, pieces=(), kind=jnp.bfloat16):
    gain = block_scale(rng, dims, pieces, -0.22, 0.18) if pieces else 1.0
    entries = jax.random.normal(rng, dims, jnp.float32) * deviation * gain
    return jnp.minimum(jnp.maximum(entries, -bound), bound).astype(kind)


def setup_inputs(seed: int = 0) -> dict:
    key_of = jax.random.split(jax.random.key(seed), 7)
    return {
        "tokens": gaussian(key_of[0], (TOKENS, D), 1.0, 6.0, ((0, 8), (1, 8))),
        "cotangent": gaussian(key_of[1], (TOKENS, D), 0.25, 1.5, ((0, 8), (1, 8))),
        "weight_in": gaussian(key_of[2], (D, FF), D ** -0.5, 0.078125, ((0, 8), (1, 12))),
        "weight_out": gaussian(key_of[3], (FF, D), FF ** -0.5, 0.0546875, ((0, 12), (1, 8))),
        "segment_ids": draw_segment_ids(jax.random.fold_in(key_of[6], 71), 0),
        "keep_mask": set_ends((jax.random.randint(key_of[5], (TOKENS,), 0, 8) < 7).astype(jnp.int32), jax.random.fold_in(key_of[5], 1), 0, 1),
    }


inv_root_two = 0.7071067811865476
inv_root_tau = 0.3989422804014327

def add_rounded(total, term):
    return total + lax.optimization_barrier(term.astype(jnp.bfloat16)).astype(jnp.float32)

def contract_cols(left, right):
    return lax.dot_general(left, right, (((1,), (1,)), ((), ())), preferred_element_type=jnp.float32)

def contract_rows(left, right):
    return lax.dot_general(left, right, (((0,), (0,)), ((), ())), preferred_element_type=jnp.float32)

def reference(tokens, cotangent, weight_in, weight_out, segment_ids, keep_mask):
    labels = jnp.arange(SEGS, dtype=jnp.int32)
    onehot = (segment_ids[:, None] == labels[None, :]).astype(jnp.float32)
    keeping = keep_mask.astype(jnp.float32)
    image_sizes = lax.optimization_barrier(jnp.sum(onehot * keeping[:, None], axis=0))
    per_token = jnp.dot(onehot, image_sizes, precision=lax.Precision.HIGHEST)
    token_weight = keeping * jnp.sqrt(IMAGE_MEAN / jnp.maximum(per_token, 1.0))
    scaled = (cotangent.astype(jnp.float32) * token_weight[:, None]).astype(jnp.bfloat16)
    width_block = D // N_ROW
    pre_act = jnp.zeros((TOKENS, FF), jnp.float32)
    back_grad = jnp.zeros((TOKENS, FF), jnp.float32)
    for bucket in range(N_ROW):
        lower = bucket * width_block
        upper = lower + width_block
        pre_act = add_rounded(pre_act, jnp.dot(tokens[:, lower:upper], weight_in[lower:upper, :], preferred_element_type=jnp.float32))
        back_grad = add_rounded(back_grad, contract_cols(scaled[:, lower:upper], weight_out[:, lower:upper]))
    normal_cdf = 0.5 * (1.0 + lax.erf(pre_act * inv_root_two))
    activation = (pre_act * normal_cdf).astype(jnp.bfloat16)
    slopes = normal_cdf + pre_act * jnp.exp(-0.5 * pre_act * pre_act) * inv_root_tau
    hidden_grad = (back_grad * slopes).astype(jnp.bfloat16)
    hidden_block = FF // N_COL
    grad_tokens = jnp.zeros((TOKENS, D), jnp.float32)
    for bucket in range(N_COL):
        lower = bucket * hidden_block
        upper = lower + hidden_block
        grad_tokens = add_rounded(grad_tokens, contract_cols(hidden_grad[:, lower:upper], weight_in[:, lower:upper]))
    token_block = TOKENS // N_BATCH
    grad_in = jnp.zeros((D, FF), jnp.float32)
    grad_out = jnp.zeros((FF, D), jnp.float32)
    for bucket in range(N_BATCH):
        lower = bucket * token_block
        upper = lower + token_block
        grad_in = add_rounded(grad_in, contract_rows(tokens[lower:upper], hidden_grad[lower:upper]))
        grad_out = add_rounded(grad_out, contract_rows(activation[lower:upper], scaled[lower:upper]))
    return (grad_tokens.astype(jnp.bfloat16), grad_in.astype(jnp.bfloat16), grad_out.astype(jnp.bfloat16))
```

```python
import functools

import jax
import jax.numpy as jnp
from jax import lax
from jax.experimental import pallas as pl
from jax.experimental.pallas import tpu as pltpu
from jax.sharding import PartitionSpec as P

SEGS = 32
IMAGE_MEAN = 128.0
MESH = pl.DeviceIdType.MESH

inv_root_two = 0.7071067811865476
inv_root_tau = 0.3989422804014327

F32 = jnp.float32
BF16 = jnp.bfloat16


def dot(left, right, lc, rc):
    return lax.dot_general(
        left, right, (((lc,), (rc,)), ((), ())), preferred_element_type=F32
    )


def gelu_parts(pre_act):
    normal_cdf = 0.5 * (1.0 + lax.erf(pre_act * inv_root_two))
    slopes = normal_cdf + pre_act * jnp.exp(-0.5 * pre_act * pre_act) * inv_root_tau
    return (pre_act * normal_cdf, slopes)


def remote(src, dst, send, recv, where):
    return pltpu.make_async_remote_copy(
        src_ref=src,
        dst_ref=dst,
        send_sem=send,
        recv_sem=recv,
        device_id=where,
        device_id_type=MESH,
    )


CHUNKS = 16
GROUPS = 2
PER = CHUNKS // GROUPS


def row_kernel(
    tokens_h, cotangent_h, w_in_h, w_out_h, hid_out,
    tokens, cotangent, w_in, w_out, snd, prt, acc, rcv, run, hid,
    pair_s, pair_r, sum_s, sum_r, back_s, back_r, side_s, side_r, out_sem, in_sem,
):
    row = lax.axis_index("row")
    core = row % 2
    z = row // 2
    place = core * z + (1 - core) * (3 - z)
    step = 4 * core - 2
    ahead = {"row": (row + step + 8) % 8}
    behind = {"row": (row - step + 8) % 8}
    partner = {"row": row + 1 - 2 * core}
    half = acc.shape[3]
    rows = acc.shape[2]
    block = PER * rows

    barrier = pltpu.get_barrier_semaphore()
    for where in (partner, ahead, behind):
        pl.semaphore_signal(barrier, inc=1, device_id=where, device_id_type=MESH)

    def columns(which):
        return pl.ds(pl.multiple_of(which * half, half), half)

    other = columns(1 - core)
    mine = columns(core)
    loads = [
        pltpu.make_async_copy(src, dst, in_sem.at[i])
        for i, (src, dst) in enumerate((
            (tokens_h, tokens),
            (w_in_h.at[:, other], w_in.at[:, other]),
            (cotangent_h, cotangent),
            (w_out_h.at[other, :], w_out.at[other, :]),
            (w_in_h.at[:, mine], w_in.at[:, mine]),
            (w_out_h.at[mine, :], w_out.at[mine, :]),
        ))
    ]
    for load in loads:
        load.start()

    def pair(g):
        part = pl.ds(g * PER, PER)
        return remote(snd.at[part], prt.at[part], pair_s.at[g], pair_r.at[g], partner)

    def products(cols, g, into, waits=()):
        toks = pl.ds(g * block, block)
        part = pl.ds(g * PER, PER)
        for i in waits[:-1]:
            loads[i].wait()
        fwd = dot(tokens[toks, :], w_in[:, cols], 1, 0)
        into[part, 0] = fwd.reshape(PER, rows, half).astype(into.dtype)
        if waits:
            loads[waits[-1]].wait()
        bwd = dot(cotangent[toks, :], w_out[cols, :], 1, 1)
        into[part, 1] = bwd.reshape(PER, rows, half).astype(into.dtype)

    loads[2].wait()
    products(other, 0, snd, (0, 1, 3))
    pl.semaphore_wait(barrier, 3)
    pair(0).start()
    products(other, 1, snd)
    pair(1).start()
    products(mine, 0, acc, (4, 5))
    products(mine, 1, acc)

    def onward(j):
        return remote(run.at[j], rcv.at[j], sum_s.at[j], sum_r.at[j], ahead)

    def back(j):
        spot = hid.at[core, j]
        return remote(spot, spot, back_s.at[j], back_r.at[j], behind)

    def side(j, which):
        spot = hid.at[which, j]
        return remote(spot, spot, side_s.at[j], side_r.at[j], partner)

    def save(j, which):
        return pltpu.make_async_copy(
            hid.at[which, j], hid_out.at[which, j], out_sem.at[which, j]
        )

    for g in range(GROUPS):
        pair(g).wait_recv()

        @pl.when(place == 0)
        def _():
            @pl.loop(g * PER, (g + 1) * PER)
            def _(j):
                run[j] = (acc[j] + prt[j].astype(F32)).astype(BF16)
                onward(j).start()

        @pl.when((place > 0) & (place < 3))
        def _():
            @pl.loop(g * PER, (g + 1) * PER)
            def _(j):
                own = acc[j] + prt[j].astype(F32)
                onward(j).wait_recv()
                run[j] = (own + rcv[j].astype(F32)).astype(BF16)
                onward(j).start()

        @pl.when(place == 3)
        def _():
            @pl.loop(g * PER, (g + 1) * PER)
            def _(j):
                onward(j).wait_recv()
                pre = acc[j, 0] + prt[j, 0].astype(F32) + rcv[j, 0].astype(F32)
                grad = acc[j, 1] + prt[j, 1].astype(F32) + rcv[j, 1].astype(F32)
                act, slopes = gelu_parts(pre)
                hid[core, j, 0] = act.astype(BF16)
                hid[core, j, 1] = (grad * slopes).astype(BF16)
                back(j).start()
                side(j, core).start()
                save(j, core).start()

    @pl.when(place < 3)
    def _():
        @pl.loop(0, CHUNKS)
        def _(j):
            back(j).wait_recv()

            @pl.when(place > 0)
            def _():
                back(j).start()

            side(j, core).start()
            save(j, core).start()

    @pl.loop(0, CHUNKS)
    def _(j):
        side(j, 1 - core).wait_recv()
        save(j, 1 - core).start()

    for g in range(GROUPS):
        pair(g).wait_send()

    @pl.loop(0, CHUNKS)
    def _(j):
        side(j, core).wait_send()
        save(j, 0).wait()
        save(j, 1).wait()

    @pl.when(place < 3)
    def _():
        @pl.loop(0, CHUNKS)
        def _(j):
            onward(j).wait_send()

    @pl.when(place > 0)
    def _():
        @pl.loop(0, CHUNKS)
        def _(j):
            back(j).wait_send()


def row_stage(tokens, cotangent, w_in, w_out):
    toks, width = tokens.shape
    cols = w_in.shape[1]
    half = cols // 2
    rows = toks // CHUNKS
    slab = (CHUNKS, 2, rows, half)
    dma = pltpu.SemaphoreType.DMA
    return pl.pallas_call(
        row_kernel,
        out_shape=jax.ShapeDtypeStruct((2,) + slab, BF16),
        in_specs=[pl.BlockSpec(memory_space=pltpu.MemorySpace.HBM)] * 4,
        out_specs=pl.BlockSpec(memory_space=pl.ANY),
        scratch_shapes=[
            pltpu.VMEM((toks, width), BF16),
            pltpu.VMEM((toks, width), BF16),
            pltpu.VMEM((width, cols), BF16),
            pltpu.VMEM((cols, width), BF16),
            pltpu.VMEM(slab, BF16),
            pltpu.VMEM(slab, BF16),
            pltpu.VMEM(slab, F32),
            pltpu.VMEM(slab, BF16),
            pltpu.VMEM(slab, BF16),
            pltpu.VMEM((2,) + slab, BF16),
            dma((GROUPS,)), dma((GROUPS,)),
            dma((CHUNKS,)), dma((CHUNKS,)),
            dma((CHUNKS,)), dma((CHUNKS,)),
            dma((CHUNKS,)), dma((CHUNKS,)),
            dma((2, CHUNKS)),
            dma((6,)),
        ],
        compiler_params=pltpu.CompilerParams(
            collective_id=0, has_side_effects=True, vmem_limit_bytes=32 << 20
        ),
        cost_estimate=pl.CostEstimate(
            flops=4 * toks * width * cols, bytes_accessed=40 << 20, transcendentals=0
        ),
        name="row_stage",
    )(tokens, cotangent, w_in, w_out)


def grad_kernel(
    n_batch, n_x, n_z,
    hid, tokens, cotangent, w_in, seg, keep,
    g_tok, g_in, g_out,
    weighted, grads, y_first, y_rest, part, x_first, x_last, z_send, z_recv, total,
    counts, counts_in,
    count_s, count_r, y_s, y_r, x_s, x_r, z_s, z_r, zg_s, zg_r, xg_s, xg_r, out_sem,
):
    b = lax.axis_index("batch")
    col = lax.axis_index("col")
    xi = col // n_z
    q = col % n_z
    half = hid.shape[4]
    toks = tokens.shape[0]
    third = part.shape[2]
    piece = grads.shape[2]
    split = piece // 2
    own_rows = toks // n_x
    own_half = own_rows // 2
    own_split = own_half // 2

    y_next = {"batch": (b + 1) % n_batch}
    y_prev = {"batch": (b + n_batch - 1) % n_batch}
    x_next = {"col": ((xi + 1) % n_x) * n_z + q}
    x_prev = {"col": ((xi + n_x - 1) % n_x) * n_z + q}
    z_one = {"col": xi * n_z + (q + 1) % n_z}
    z_two = {"col": xi * n_z + (q + 2) % n_z}
    y_to = (y_next, y_prev)
    x_to = (x_next, x_prev)
    z_to = (z_one, z_two)

    barrier = pltpu.get_barrier_semaphore()
    for where in y_to + x_to + z_to:
        pl.semaphore_signal(barrier, inc=1, device_id=where, device_id_type=MESH)

    labels = lax.broadcasted_iota(jnp.int32, (SEGS, toks), 0)
    marks = jnp.where((labels == seg[...]) & (keep[...] == 1), 1.0, 0.0).astype(F32)
    counts[...] = jnp.broadcast_to(
        jnp.sum(marks, axis=1, keepdims=True), counts.shape
    )
    pl.semaphore_wait(barrier, 6)

    def count_copy(d):
        return remote(counts, counts_in.at[d], count_s.at[d], count_r.at[d], y_to[d])

    count_copy(0).start()
    count_copy(1).start()

    def hidden(h, a):
        return hid[h, :, a].reshape(toks, half)

    raw = []
    for i in range(3):
        rows = pl.ds(i * third, third)
        raw.append(
            dot(hidden(0, 1), w_in[rows, 0:half], 1, 1)
            + dot(hidden(1, 1), w_in[rows, half:2 * half], 1, 1)
        )
    count_copy(0).wait_recv()
    count_copy(1).wait_recv()
    sizes = counts[...] + counts_in[0] + counts_in[1]
    sizes = jnp.concatenate([sizes, sizes], axis=1)
    per_token = dot(marks, sizes, 0, 0)
    weight = jnp.where(
        per_token > 0.0, jnp.sqrt(IMAGE_MEAN / jnp.maximum(per_token, 1.0)), 0.0
    )
    for i in range(3):
        part[i] = (raw[i] * weight).astype(BF16)

    def rows_of(ref, owner, start, size):
        first = pl.multiple_of(owner * own_rows + start, size)
        return ref.at[:, pl.ds(first, size), :]

    x_far = (xi + 2) % n_x
    x_near = ((xi + 1) % n_x, (xi + n_x - 1) % n_x)

    def x_sum(u, s, d):
        start = u * own_half
        if s == 0:
            src = rows_of(part, x_far, start + d * own_split, own_split)
            dst = x_first.at[u, d]
        else:
            src = rows_of(part, x_near[d], start, own_half)
            dst = x_last.at[u, d]
        return remote(src, dst, x_s.at[u, s, d], x_r.at[u, s, d], x_to[d])

    for u in range(2):
        x_sum(u, 0, 0).start()
        x_sum(u, 0, 1).start()

    def y_owner(s, d):
        shift = 4 - s
        return (b + shift) % n_batch if d == 0 else (b + n_batch - shift) % n_batch

    def y_sum(a, s, d):
        src = grads.at[a, y_owner(s, d)]
        if s == 0:
            src = src.at[pl.ds(d * split, split), :]
            dst = y_first.at[a, d]
        else:
            dst = y_rest.at[a, d, s - 1]
        return remote(src, dst, y_s.at[a, s, d], y_r.at[a, s, d], y_to[d])

    def products(a, source):
        for i in range(3):
            lanes = pl.ds(i * third, third)
            weighted[:, lanes] = (source[:, lanes].astype(F32) * weight).astype(BF16)
        for h in range(2):
            block = dot(weighted[...], hidden(h, 1 - a), 0, 0)
            grads[a, :, :, h * half:(h + 1) * half] = block.reshape(
                n_batch, piece, half
            ).astype(BF16)
        y_sum(a, 0, 0).start()
        y_sum(a, 0, 1).start()

    def y_onward(a, s):
        for d in range(2):
            y_sum(a, s - 1, d).wait_recv()
            owner = y_owner(s, d)
            if s == 1:
                lines = pl.ds(d * split, split)
                grads[a, owner, lines, :] = (
                    grads[a, owner, lines, :].astype(F32) + y_first[a, d].astype(F32)
                ).astype(BF16)
            else:
                grads[a, owner] = (
                    grads[a, owner].astype(F32) + y_rest[a, d, s - 2].astype(F32)
                ).astype(BF16)
            y_sum(a, s, d).start()

    def y_finish(a, out):
        y_sum(a, 3, 0).wait_recv()
        y_sum(a, 3, 1).wait_recv()
        out[...] = (
            grads[a, b].astype(F32)
            + y_rest[a, 0, 2].astype(F32)
            + y_rest[a, 1, 2].astype(F32)
        ).astype(BF16)

    def x_onward(u):
        for d in range(2):
            x_sum(u, 0, d).wait_recv()
            first = x_near[d] * own_rows + u * own_half + d * own_split
            lines = pl.ds(pl.multiple_of(first, own_split), own_split)
            part[:, lines, :] = (
                part[:, lines, :].astype(F32) + x_first[u, d].astype(F32)
            ).astype(BF16)
            x_sum(u, 1, d).start()

    def z_sum(u, k):
        target = (q + 1 + k) % n_z
        return remote(
            z_send.at[u, target], z_recv.at[u, k], z_s.at[u, k], z_r.at[u, k], z_to[k]
        )

    def mine(u):
        return pl.ds(pl.multiple_of(xi * own_rows + u * own_half, own_half), own_half)

    def z_scatter(u):
        x_sum(u, 1, 0).wait_recv()
        x_sum(u, 1, 1).wait_recv()
        z_send[u] = (
            part[:, mine(u), :].astype(F32)
            + x_last[u, 0].astype(F32)
            + x_last[u, 1].astype(F32)
        ).astype(BF16)
        z_sum(u, 0).start()
        z_sum(u, 1).start()

    def z_give(u, k):
        spot = total.at[q, mine(u), :]
        return remote(spot, spot, zg_s.at[u, k], zg_r.at[u, k], z_to[k])

    def z_gather(u):
        z_sum(u, 0).wait_recv()
        z_sum(u, 1).wait_recv()
        total[q, mine(u), :] = (
            z_send[u, q].astype(F32)
            + z_recv[u, 0].astype(F32)
            + z_recv[u, 1].astype(F32)
        ).astype(BF16)
        z_give(u, 0).start()
        z_give(u, 1).start()

    def x_give(u, s, d):
        start = u * own_half
        if s == 0:
            spot = rows_of(total, xi, start, own_half)
        else:
            spot = rows_of(total, x_near[1 - d], start + d * own_split, own_split)
        return remote(spot, spot, xg_s.at[u, s, d], xg_r.at[u, s, d], x_to[d])

    def x_gather(u):
        z_give(u, 0).wait_recv()
        z_give(u, 1).wait_recv()
        x_give(u, 0, 0).start()
        x_give(u, 0, 1).start()

    def x_forward(u):
        for d in range(2):
            x_give(u, 0, d).wait_recv()
            x_give(u, 1, d).start()

    def save(i):
        return pltpu.make_async_copy(
            total.at[i], g_tok.at[:, pl.ds(i * third, third)], out_sem.at[i]
        )

    products(1, cotangent)
    x_onward(0)
    x_onward(1)
    products(0, tokens)
    z_scatter(0)
    y_onward(1, 1)
    z_scatter(1)
    y_onward(0, 1)
    z_gather(0)
    y_onward(1, 2)
    z_gather(1)
    y_onward(0, 2)
    x_gather(0)
    y_onward(1, 3)
    x_gather(1)
    x_forward(0)
    y_onward(0, 3)
    x_forward(1)
    y_finish(1, g_out)
    for u in range(2):
        x_give(u, 1, 0).wait_recv()
        x_give(u, 1, 1).wait_recv()
    for i in range(3):
        save(i).start()
    y_finish(0, g_in)

    for d in range(2):
        count_copy(d).wait_send()
        for u in range(2):
            z_sum(u, d).wait_send()
            z_give(u, d).wait_send()
            for s in range(2):
                x_sum(u, s, d).wait_send()
                x_give(u, s, d).wait_send()
        for s in range(4):
            for a in range(2):
                y_sum(a, s, d).wait_send()
    for i in range(3):
        save(i).wait()


def grad_stage(mesh_shape, hid, tokens, cotangent, w_in, seg, keep):
    n_batch = mesh_shape["batch"]
    n_x, n_z = 4, mesh_shape["col"] // 4
    toks, width = tokens.shape
    cols = w_in.shape[1]
    third = width // 3
    piece = width // n_batch
    own = toks // n_x
    dma = pltpu.SemaphoreType.DMA
    vmem = pl.BlockSpec(memory_space=pltpu.VMEM)
    return pl.pallas_call(
        functools.partial(grad_kernel, n_batch, n_x, n_z),
        out_shape=(
            jax.ShapeDtypeStruct((toks, width), BF16),
            jax.ShapeDtypeStruct((piece, cols), BF16),
            jax.ShapeDtypeStruct((piece, cols), BF16),
        ),
        in_specs=[vmem] * 6,
        out_specs=(pl.BlockSpec(memory_space=pl.ANY), vmem, vmem),
        scratch_shapes=[
            pltpu.VMEM((toks, width), BF16),
            pltpu.VMEM((2, n_batch, piece, cols), BF16),
            pltpu.VMEM((2, 2, piece // 2, cols), BF16),
            pltpu.VMEM((2, 2, 3, piece, cols), BF16),
            pltpu.VMEM((3, toks, third), BF16),
            pltpu.VMEM((2, 2, 3, own // 4, third), BF16),
            pltpu.VMEM((2, 2, 3, own // 2, third), BF16),
            pltpu.VMEM((2, 3, own // 2, third), BF16),
            pltpu.VMEM((2, 2, own // 2, third), BF16),
            pltpu.VMEM((3, toks, third), BF16),
            pltpu.VMEM((SEGS, 128), F32),
            pltpu.VMEM((2, SEGS, 128), F32),
            dma((2,)), dma((2,)),
            dma((2, 4, 2)), dma((2, 4, 2)),
            dma((2, 2, 2)), dma((2, 2, 2)),
            dma((2, 2)), dma((2, 2)),
            dma((2, 2)), dma((2, 2)),
            dma((2, 2, 2)), dma((2, 2, 2)),
            dma((3,)),
        ],
        compiler_params=pltpu.CompilerParams(
            collective_id=1, has_side_effects=True, vmem_limit_bytes=40 << 20
        ),
        cost_estimate=pl.CostEstimate(
            flops=6 * toks * width * cols, bytes_accessed=40 << 20, transcendentals=0
        ),
        name="grad_stage",
    )(hid, tokens, cotangent, w_in, seg, keep)


def per_device(mesh_shape, tokens, cotangent, weight_in, weight_out, segment_ids, keep_mask):
    hid = row_stage(*(
        pltpu.with_memory_space_constraint(x, pltpu.MemorySpace.HBM)
        for x in (tokens, cotangent, weight_in, weight_out)
    ))
    grad_tokens, grad_in, grad_out = grad_stage(
        mesh_shape, hid, tokens, cotangent, weight_in,
        segment_ids[None, :], keep_mask[None, :],
    )
    return (grad_tokens, grad_in, grad_out.T)


def solution(mesh):
    return jax.shard_map(
        functools.partial(per_device, dict(mesh.shape)),
        mesh=mesh,
        in_specs=(
            P("batch", "row"),
            P("batch", "row"),
            P("row", "col"),
            P("col", "row"),
            P("batch"),
            P("batch"),
        ),
        out_specs=(P("batch", "row"), P(("row", "batch"), "col"), P("col", ("row", "batch"))),
        check_vma=False,
    )
```

```python
import functools

import jax
import jax.numpy as jnp
from jax import lax
from jax.experimental import pallas as pl
from jax.experimental.pallas import tpu as pltpu
from jax.sharding import PartitionSpec as P

SEGS = 32
IMAGE_MEAN = 128.0
MESH = pl.DeviceIdType.MESH

inv_root_two = 0.7071067811865476
inv_root_tau = 0.3989422804014327

F32 = jnp.float32
BF16 = jnp.bfloat16


def dot(left, right, lc, rc):
    return lax.dot_general(
        left, right, (((lc,), (rc,)), ((), ())), preferred_element_type=F32
    )


def gelu_parts(pre_act):
    normal_cdf = 0.5 * (1.0 + lax.erf(pre_act * inv_root_two))
    slopes = normal_cdf + pre_act * jnp.exp(-0.5 * pre_act * pre_act) * inv_root_tau
    return (pre_act * normal_cdf, slopes)


def remote(src, dst, send, recv, where):
    return pltpu.make_async_remote_copy(
        src_ref=src,
        dst_ref=dst,
        send_sem=send,
        recv_sem=recv,
        device_id=where,
        device_id_type=MESH,
    )


GROUPS = 2
PER = 8
CHUNKS = GROUPS * PER


def row_kernel(
    n_batch,
    tokens_h, cotangent_h, w_in_h, w_out_h, seg_h, keep_h,
    hid_out, w_tok_out, w_cot_out, weight_out,
    tokens, cotangent, w_in, w_out, seg, keep,
    snd, prt, acc, rcv, run, hid,
    w_tok, w_cot, weights, counts, counts_in,
    pair_s, pair_r, sum_s, sum_r, back_s, back_r, side_s, side_r,
    count_s, count_r, out_sem, in_sem, w_sem,
):
    b = lax.axis_index("batch")
    row = lax.axis_index("row")
    core = row % 2
    z = row // 2
    place = core * z + (1 - core) * (3 - z)
    step = 4 * core - 2
    ahead = {"row": (row + step + 8) % 8}
    behind = {"row": (row - step + 8) % 8}
    partner = {"row": row + 1 - 2 * core}
    y_to = ({"batch": (b + 1) % n_batch}, {"batch": (b + n_batch - 1) % n_batch})
    rows, wide = acc.shape[2], acc.shape[3]
    toks, width = tokens.shape
    half = GROUPS * wide

    barrier = pltpu.get_barrier_semaphore()
    for where in (partner, ahead, behind) + y_to:
        pl.semaphore_signal(barrier, inc=1, device_id=where, device_id_type=MESH)

    def columns(which):
        return pl.ds(pl.multiple_of(which * half, half), half)

    other = columns(1 - core)
    mine = columns(core)
    loads = [
        pltpu.make_async_copy(src, dst, in_sem.at[i])
        for i, (src, dst) in enumerate((
            (seg_h, seg),
            (keep_h, keep),
            (tokens_h, tokens),
            (w_in_h.at[:, other], w_in.at[:, other]),
            (cotangent_h, cotangent),
            (w_out_h.at[other, :], w_out.at[other, :]),
            (w_in_h.at[:, mine], w_in.at[:, mine]),
            (w_out_h.at[mine, :], w_out.at[mine, :]),
        ))
    ]
    for load in loads:
        load.start()

    loads[0].wait()
    loads[1].wait()
    labels = lax.broadcasted_iota(jnp.int32, (SEGS, toks), 0)

    def image_marks():
        return jnp.where((labels == seg[...]) & (keep[...] == 1), 1.0, 0.0).astype(F32)

    counts[...] = jnp.broadcast_to(
        jnp.sum(image_marks(), axis=1, keepdims=True), counts.shape
    )

    def count_copy(d):
        return remote(counts, counts_in.at[d], count_s.at[d], count_r.at[d], y_to[d])

    def pair(g):
        part = pl.ds(g * PER, PER)
        return remote(snd.at[part], prt.at[part], pair_s.at[g], pair_r.at[g], partner)

    def products(which, g, into):
        cols = pl.ds(pl.multiple_of(which * half + g * wide, wide), wide)
        part = pl.ds(g * PER, PER)
        fwd = dot(tokens[...], w_in[:, cols], 1, 0)
        into[part, 0] = fwd.reshape(PER, rows, wide).astype(into.dtype)
        bwd = dot(cotangent[...], w_out[cols, :], 1, 1)
        into[part, 1] = bwd.reshape(PER, rows, wide).astype(into.dtype)

    def onward(j):
        return remote(run.at[j], rcv.at[j], sum_s.at[j], sum_r.at[j], ahead)

    def back(j):
        spot = hid.at[core, j]
        return remote(spot, spot, back_s.at[j], back_r.at[j], behind)

    def side(j, which):
        spot = hid.at[which, j]
        return remote(spot, spot, side_s.at[j], side_r.at[j], partner)

    def save(j, which):
        return pltpu.make_async_copy(
            hid.at[which, j], hid_out.at[which, j], out_sem.at[which, j]
        )

    def begin(g):
        @pl.when(place == 0)
        def _():
            pair(g).wait_recv()

            @pl.loop(g * PER, (g + 1) * PER)
            def _(j):
                run[j] = (acc[j] + prt[j].astype(F32)).astype(BF16)
                onward(j).start()

    for load in loads[2:6]:
        load.wait()
    products(1 - core, 0, snd)
    pl.semaphore_wait(barrier, 5)
    pair(0).start()
    count_copy(0).start()
    count_copy(1).start()
    products(1 - core, 1, snd)
    pair(1).start()
    loads[6].wait()
    loads[7].wait()
    products(core, 0, acc)
    begin(0)
    products(core, 1, acc)
    begin(1)

    count_copy(0).wait_recv()
    count_copy(1).wait_recv()
    sizes = counts[...] + counts_in[0] + counts_in[1]
    sizes = jnp.concatenate([sizes, sizes], axis=1)
    per_token = dot(image_marks(), sizes, 0, 0)
    weight = jnp.where(
        per_token > 0.0, jnp.sqrt(IMAGE_MEAN / jnp.maximum(per_token, 1.0)), 0.0
    )
    weights[...] = weight
    span = weight.shape[1]
    for i in range(width // span):
        lanes = pl.ds(i * span, span)
        w_tok[:, lanes] = (tokens[:, lanes].astype(F32) * weight).astype(BF16)
        w_cot[:, lanes] = (cotangent[:, lanes].astype(F32) * weight).astype(BF16)
    keeps = [
        pltpu.make_async_copy(src, dst, w_sem.at[i])
        for i, (src, dst) in enumerate((
            (w_tok, w_tok_out), (w_cot, w_cot_out), (weights, weight_out),
        ))
    ]
    for copy in keeps:
        copy.start()

    for g in range(GROUPS):
        @pl.when((place > 0) & (place < 3))
        def _():
            pair(g).wait_recv()

            @pl.loop(g * PER, (g + 1) * PER)
            def _(j):
                own = acc[j] + prt[j].astype(F32)
                onward(j).wait_recv()
                run[j] = (own + rcv[j].astype(F32)).astype(BF16)
                onward(j).start()

        @pl.when(place == 3)
        def _():
            pair(g).wait_recv()

            @pl.loop(g * PER, (g + 1) * PER)
            def _(j):
                onward(j).wait_recv()
                pre = acc[j, 0] + prt[j, 0].astype(F32) + rcv[j, 0].astype(F32)
                grad = acc[j, 1] + prt[j, 1].astype(F32) + rcv[j, 1].astype(F32)
                act, slopes = gelu_parts(pre)
                hid[core, j, 0] = act.astype(BF16)
                hid[core, j, 1] = (grad * slopes).astype(BF16)
                back(j).start()
                side(j, core).start()
                save(j, core).start()

    @pl.when(place < 3)
    def _():
        @pl.loop(0, CHUNKS)
        def _(j):
            back(j).wait_recv()

            @pl.when(place > 0)
            def _():
                back(j).start()

            side(j, core).start()
            save(j, core).start()

    @pl.loop(0, CHUNKS)
    def _(j):
        side(j, 1 - core).wait_recv()
        save(j, 1 - core).start()

    for g in range(GROUPS):
        pair(g).wait_send()
        count_copy(g).wait_send()
    for copy in keeps:
        copy.wait()

    @pl.loop(0, CHUNKS)
    def _(j):
        side(j, core).wait_send()
        save(j, 0).wait()
        save(j, 1).wait()

    @pl.when(place < 3)
    def _():
        @pl.loop(0, CHUNKS)
        def _(j):
            onward(j).wait_send()

    @pl.when(place > 0)
    def _():
        @pl.loop(0, CHUNKS)
        def _(j):
            back(j).wait_send()


def row_stage(mesh_shape, tokens, cotangent, w_in, w_out, seg, keep):
    toks, width = tokens.shape
    cols = w_in.shape[1]
    slab = (CHUNKS, 2, toks // PER, cols // 2 // GROUPS)
    dma = pltpu.SemaphoreType.DMA
    args = [
        pltpu.with_memory_space_constraint(x, pltpu.MemorySpace.HBM)
        for x in (tokens, cotangent, w_in, w_out, seg, keep)
    ]
    return pl.pallas_call(
        functools.partial(row_kernel, mesh_shape["batch"]),
        out_shape=(
            jax.ShapeDtypeStruct((2,) + slab, BF16),
            jax.ShapeDtypeStruct((toks, width), BF16),
            jax.ShapeDtypeStruct((toks, width), BF16),
            jax.ShapeDtypeStruct((toks, 256), F32),
        ),
        in_specs=[pl.BlockSpec(memory_space=pltpu.MemorySpace.HBM)] * 6,
        out_specs=(pl.BlockSpec(memory_space=pl.ANY),) * 4,
        scratch_shapes=[
            pltpu.VMEM((toks, width), BF16),
            pltpu.VMEM((toks, width), BF16),
            pltpu.VMEM((width, cols), BF16),
            pltpu.VMEM((cols, width), BF16),
            pltpu.VMEM((1, toks), jnp.int32),
            pltpu.VMEM((1, toks), jnp.int32),
            pltpu.VMEM(slab, BF16),
            pltpu.VMEM(slab, BF16),
            pltpu.VMEM(slab, F32),
            pltpu.VMEM(slab, BF16),
            pltpu.VMEM(slab, BF16),
            pltpu.VMEM((2,) + slab, BF16),
            pltpu.VMEM((toks, width), BF16),
            pltpu.VMEM((toks, width), BF16),
            pltpu.VMEM((toks, 256), F32),
            pltpu.VMEM((SEGS, 128), F32),
            pltpu.VMEM((2, SEGS, 128), F32),
            dma((GROUPS,)), dma((GROUPS,)),
            dma((CHUNKS,)), dma((CHUNKS,)),
            dma((CHUNKS,)), dma((CHUNKS,)),
            dma((CHUNKS,)), dma((CHUNKS,)),
            dma((2,)), dma((2,)),
            dma((2, CHUNKS)), dma((8,)), dma((3,)),
        ],
        compiler_params=pltpu.CompilerParams(
            collective_id=0, has_side_effects=True, vmem_limit_bytes=36 << 20
        ),
        cost_estimate=pl.CostEstimate(
            flops=4 * toks * width * cols, bytes_accessed=40 << 20, transcendentals=0
        ),
        name="row_stage",
    )(*args)


def grad_kernel(
    n_batch, n_x, n_z,
    hid, w_tok, w_cot, w_in, weights,
    g_tok, g_in, g_out,
    grads, y_first, y_rest, part, x_first, x_last, z_send, z_recv, total,
    y_s, y_r, x_s, x_r, z_s, z_r, zg_s, zg_r, xg_s, xg_r, out_sem,
):
    b = lax.axis_index("batch")
    col = lax.axis_index("col")
    xi = col // n_z
    q = col % n_z
    wide = hid.shape[4]
    toks = w_tok.shape[0]
    third = part.shape[2]
    piece = grads.shape[2]
    split = piece // 2
    own_rows = toks // n_x
    own_half = own_rows // 2
    own_split = own_half // 2

    y_next = {"batch": (b + 1) % n_batch}
    y_prev = {"batch": (b + n_batch - 1) % n_batch}
    x_next = {"col": ((xi + 1) % n_x) * n_z + q}
    x_prev = {"col": ((xi + n_x - 1) % n_x) * n_z + q}
    z_one = {"col": xi * n_z + (q + 1) % n_z}
    z_two = {"col": xi * n_z + (q + 2) % n_z}
    y_to = (y_next, y_prev)
    x_to = (x_next, x_prev)
    z_to = (z_one, z_two)

    barrier = pltpu.get_barrier_semaphore()
    for where in y_to + x_to + z_to:
        pl.semaphore_signal(barrier, inc=1, device_id=where, device_id_type=MESH)

    blocks = [(h, g) for h in range(2) for g in range(GROUPS)]

    def hidden(h, g, a):
        return hid[h, g * PER:(g + 1) * PER, a].reshape(toks, wide)

    def place(h, g):
        first = (h * GROUPS + g) * wide
        return slice(first, first + wide)

    def rows_of(ref, owner, start, size):
        first = pl.multiple_of(owner * own_rows + start, size)
        return ref.at[:, pl.ds(first, size), :]

    x_far = (xi + 2) % n_x
    x_near = ((xi + 1) % n_x, (xi + n_x - 1) % n_x)

    def x_sum(u, s, d):
        start = u * own_half
        if s == 0:
            src = rows_of(part, x_far, start + d * own_split, own_split)
            dst = x_first.at[u, d]
        else:
            src = rows_of(part, x_near[d], start, own_half)
            dst = x_last.at[u, d]
        return remote(src, dst, x_s.at[u, s, d], x_r.at[u, s, d], x_to[d])

    def y_owner(s, d):
        shift = 4 - s
        return (b + shift) % n_batch if d == 0 else (b + n_batch - shift) % n_batch

    def y_sum(a, s, d):
        src = grads.at[a, y_owner(s, d)]
        if s == 0:
            src = src.at[pl.ds(d * split, split), :]
            dst = y_first.at[a, d]
        else:
            dst = y_rest.at[a, d, s - 1]
        return remote(src, dst, y_s.at[a, s, d], y_r.at[a, s, d], y_to[d])

    def products(a, source):
        for h, g in blocks:
            block = dot(source[...], hidden(h, g, 1 - a), 0, 0)
            grads[a, :, :, place(h, g)] = block.reshape(n_batch, piece, wide).astype(BF16)

    def y_begin(a):
        y_sum(a, 0, 0).start()
        y_sum(a, 0, 1).start()

    def input_products():
        for i in range(3):
            rows = pl.ds(i * third, third)
            raw = sum(
                dot(hidden(h, g, 1), w_in[rows, place(h, g)], 1, 1) for h, g in blocks
            )
            part[i] = (raw * weights[...]).astype(BF16)
        for u in range(2):
            x_sum(u, 0, 0).start()
            x_sum(u, 0, 1).start()

    def y_onward(a, s):
        for d in range(2):
            y_sum(a, s - 1, d).wait_recv()
            owner = y_owner(s, d)
            if s == 1:
                lines = pl.ds(d * split, split)
                grads[a, owner, lines, :] = (
                    grads[a, owner, lines, :].astype(F32) + y_first[a, d].astype(F32)
                ).astype(BF16)
            else:
                grads[a, owner] = (
                    grads[a, owner].astype(F32) + y_rest[a, d, s - 2].astype(F32)
                ).astype(BF16)
            y_sum(a, s, d).start()

    def y_finish(a, out):
        y_sum(a, 3, 0).wait_recv()
        y_sum(a, 3, 1).wait_recv()
        out[...] = (
            grads[a, b].astype(F32)
            + y_rest[a, 0, 2].astype(F32)
            + y_rest[a, 1, 2].astype(F32)
        ).astype(BF16)

    def x_onward(u):
        for d in range(2):
            x_sum(u, 0, d).wait_recv()
            first = x_near[d] * own_rows + u * own_half + d * own_split
            lines = pl.ds(pl.multiple_of(first, own_split), own_split)
            part[:, lines, :] = (
                part[:, lines, :].astype(F32) + x_first[u, d].astype(F32)
            ).astype(BF16)
            x_sum(u, 1, d).start()

    def z_sum(u, k):
        target = (q + 1 + k) % n_z
        return remote(
            z_send.at[u, target], z_recv.at[u, k], z_s.at[u, k], z_r.at[u, k], z_to[k]
        )

    def mine(u):
        return pl.ds(pl.multiple_of(xi * own_rows + u * own_half, own_half), own_half)

    def z_scatter(u):
        x_sum(u, 1, 0).wait_recv()
        x_sum(u, 1, 1).wait_recv()
        z_send[u] = (
            part[:, mine(u), :].astype(F32)
            + x_last[u, 0].astype(F32)
            + x_last[u, 1].astype(F32)
        ).astype(BF16)
        z_sum(u, 0).start()
        z_sum(u, 1).start()

    def z_give(u, k):
        spot = total.at[q, mine(u), :]
        return remote(spot, spot, zg_s.at[u, k], zg_r.at[u, k], z_to[k])

    def z_gather(u):
        z_sum(u, 0).wait_recv()
        z_sum(u, 1).wait_recv()
        total[q, mine(u), :] = (
            z_send[u, q].astype(F32)
            + z_recv[u, 0].astype(F32)
            + z_recv[u, 1].astype(F32)
        ).astype(BF16)
        z_give(u, 0).start()
        z_give(u, 1).start()

    def x_give(u, s, d):
        start = u * own_half
        if s == 0:
            spot = rows_of(total, xi, start, own_half)
        else:
            spot = rows_of(total, x_near[1 - d], start + d * own_split, own_split)
        return remote(spot, spot, xg_s.at[u, s, d], xg_r.at[u, s, d], x_to[d])

    def x_gather(u):
        z_give(u, 0).wait_recv()
        z_give(u, 1).wait_recv()
        x_give(u, 0, 0).start()
        x_give(u, 0, 1).start()

    def x_forward(u):
        for d in range(2):
            x_give(u, 0, d).wait_recv()
            x_give(u, 1, d).start()

    def save(i):
        return pltpu.make_async_copy(
            total.at[i], g_tok.at[:, pl.ds(i * third, third)], out_sem.at[i]
        )

    products(1, w_cot)
    pl.semaphore_wait(barrier, 6)
    y_begin(1)
    input_products()
    products(0, w_tok)
    y_begin(0)
    x_onward(0)
    x_onward(1)
    z_scatter(0)
    y_onward(1, 1)
    z_scatter(1)
    y_onward(0, 1)
    z_gather(0)
    y_onward(1, 2)
    z_gather(1)
    y_onward(0, 2)
    x_gather(0)
    y_onward(1, 3)
    x_gather(1)
    x_forward(0)
    y_onward(0, 3)
    x_forward(1)
    y_finish(1, g_out)
    for u in range(2):
        x_give(u, 1, 0).wait_recv()
        x_give(u, 1, 1).wait_recv()
    for i in range(3):
        save(i).start()
    y_finish(0, g_in)

    for d in range(2):
        for u in range(2):
            z_sum(u, d).wait_send()
            z_give(u, d).wait_send()
            for s in range(2):
                x_sum(u, s, d).wait_send()
                x_give(u, s, d).wait_send()
        for s in range(4):
            for a in range(2):
                y_sum(a, s, d).wait_send()
    for i in range(3):
        save(i).wait()


def grad_stage(mesh_shape, hid, w_tok, w_cot, w_in, weights):
    n_batch = mesh_shape["batch"]
    n_x, n_z = 4, mesh_shape["col"] // 4
    toks, width = w_tok.shape
    cols = w_in.shape[1]
    third = width // 3
    piece = width // n_batch
    own = toks // n_x
    dma = pltpu.SemaphoreType.DMA
    vmem = pl.BlockSpec(memory_space=pltpu.VMEM)
    return pl.pallas_call(
        functools.partial(grad_kernel, n_batch, n_x, n_z),
        out_shape=(
            jax.ShapeDtypeStruct((toks, width), BF16),
            jax.ShapeDtypeStruct((piece, cols), BF16),
            jax.ShapeDtypeStruct((piece, cols), BF16),
        ),
        in_specs=[vmem] * 5,
        out_specs=(pl.BlockSpec(memory_space=pl.ANY), vmem, vmem),
        scratch_shapes=[
            pltpu.VMEM((2, n_batch, piece, cols), BF16),
            pltpu.VMEM((2, 2, piece // 2, cols), BF16),
            pltpu.VMEM((2, 2, 3, piece, cols), BF16),
            pltpu.VMEM((3, toks, third), BF16),
            pltpu.VMEM((2, 2, 3, own // 4, third), BF16),
            pltpu.VMEM((2, 2, 3, own // 2, third), BF16),
            pltpu.VMEM((2, 3, own // 2, third), BF16),
            pltpu.VMEM((2, 2, own // 2, third), BF16),
            pltpu.VMEM((3, toks, third), BF16),
            dma((2, 4, 2)), dma((2, 4, 2)),
            dma((2, 2, 2)), dma((2, 2, 2)),
            dma((2, 2)), dma((2, 2)),
            dma((2, 2)), dma((2, 2)),
            dma((2, 2, 2)), dma((2, 2, 2)),
            dma((3,)),
        ],
        compiler_params=pltpu.CompilerParams(
            collective_id=1, has_side_effects=True, vmem_limit_bytes=36 << 20
        ),
        cost_estimate=pl.CostEstimate(
            flops=6 * toks * width * cols, bytes_accessed=40 << 20, transcendentals=0
        ),
        name="grad_stage",
    )(hid, w_tok, w_cot, w_in, weights)


def publish_kernel(*refs):
    count = (len(refs) - 1) // 2
    copies = [
        pltpu.make_async_copy(refs[i], refs[count + i], refs[-1].at[i])
        for i in range(count)
    ]
    for copy in copies:
        copy.start()
    for copy in copies:
        copy.wait()


def publish(*arrays):
    anywhere = pl.BlockSpec(memory_space=pl.ANY)
    return pl.pallas_call(
        publish_kernel,
        out_shape=tuple(jax.ShapeDtypeStruct(x.shape, x.dtype) for x in arrays),
        in_specs=[anywhere] * len(arrays),
        out_specs=(anywhere,) * len(arrays),
        scratch_shapes=[pltpu.SemaphoreType.DMA((len(arrays),))],
        compiler_params=pltpu.CompilerParams(vmem_limit_bytes=8 << 20),
        name="publish",
    )(*arrays)


def per_device(mesh_shape, tokens, cotangent, weight_in, weight_out, segment_ids, keep_mask):
    hid, w_tok, w_cot, weights = row_stage(
        mesh_shape, tokens, cotangent, weight_in, weight_out,
        segment_ids[None, :], keep_mask[None, :],
    )
    grad_tokens, grad_in, grad_out = publish(
        *grad_stage(mesh_shape, hid, w_tok, w_cot, weight_in, weights)
    )
    return (grad_tokens, grad_in, grad_out.T)


def solution(mesh):
    return jax.shard_map(
        functools.partial(per_device, dict(mesh.shape)),
        mesh=mesh,
        in_specs=(
            P("batch", "row"),
            P("batch", "row"),
            P("row", "col"),
            P("col", "row"),
            P("batch"),
            P("batch"),
        ),
        out_specs=(P("batch", "row"), P(("row", "batch"), "col"), P("col", ("row", "batch"))),
        check_vma=False,
    )
```

```python
import functools

import jax
import jax.numpy as jnp
from jax import lax
from jax.experimental import pallas as pl
from jax.experimental.pallas import tpu as pltpu
from jax.sharding import PartitionSpec as P

SEGS = 32
IMAGE_MEAN = 128.0
MESH = pl.DeviceIdType.MESH

inv_root_two = 0.7071067811865476
inv_root_tau = 0.3989422804014327

F32 = jnp.float32
BF16 = jnp.bfloat16


def dot(left, right, lc, rc):
    return lax.dot_general(
        left, right, (((lc,), (rc,)), ((), ())), preferred_element_type=F32
    )


def gelu_parts(pre_act):
    normal_cdf = 0.5 * (1.0 + lax.erf(pre_act * inv_root_two))
    slopes = normal_cdf + pre_act * jnp.exp(-0.5 * pre_act * pre_act) * inv_root_tau
    return (pre_act * normal_cdf, slopes)


def remote(src, dst, send, recv, where):
    return pltpu.make_async_remote_copy(
        src_ref=src,
        dst_ref=dst,
        send_sem=send,
        recv_sem=recv,
        device_id=where,
        device_id_type=MESH,
    )


GROUPS = 2
PER = 8
CHUNKS = GROUPS * PER


def row_kernel(
    n_batch,
    tokens_h, cotangent_h, w_in_h, w_out_h, seg_h, keep_h,
    hid_out, w_tok_out, w_cot_out, weight_out,
    tokens, cotangent, w_in, w_out, seg, keep,
    snd, prt, acc, rcv, run, hid,
    w_tok, w_cot, weights, counts, counts_in,
    pair_s, pair_r, sum_s, sum_r, back_s, back_r, side_s, side_r,
    count_s, count_r, out_sem, in_sem, w_sem,
):
    b = lax.axis_index("batch")
    row = lax.axis_index("row")
    core = row % 2
    z = row // 2
    place = core * z + (1 - core) * (3 - z)
    step = 4 * core - 2
    ahead = {"row": (row + step + 8) % 8}
    behind = {"row": (row - step + 8) % 8}
    partner = {"row": row + 1 - 2 * core}
    y_to = ({"batch": (b + 1) % n_batch}, {"batch": (b + n_batch - 1) % n_batch})
    rows, wide = acc.shape[2], acc.shape[3]
    toks, width = tokens.shape
    half = GROUPS * wide

    barrier = pltpu.get_barrier_semaphore()
    for where in (partner, ahead, behind) + y_to:
        pl.semaphore_signal(barrier, inc=1, device_id=where, device_id_type=MESH)

    def columns(which):
        return pl.ds(pl.multiple_of(which * half, half), half)

    other = columns(1 - core)
    mine = columns(core)
    loads = [
        pltpu.make_async_copy(src, dst, in_sem.at[i])
        for i, (src, dst) in enumerate((
            (seg_h, seg),
            (keep_h, keep),
            (tokens_h, tokens),
            (w_in_h.at[:, other], w_in.at[:, other]),
            (cotangent_h, cotangent),
            (w_out_h.at[other, :], w_out.at[other, :]),
            (w_in_h.at[:, mine], w_in.at[:, mine]),
            (w_out_h.at[mine, :], w_out.at[mine, :]),
        ))
    ]
    for load in loads:
        load.start()

    loads[0].wait()
    loads[1].wait()
    labels = lax.broadcasted_iota(jnp.int32, (SEGS, toks), 0)

    def image_marks():
        return jnp.where((labels == seg[...]) & (keep[...] == 1), 1.0, 0.0).astype(F32)

    counts[...] = jnp.broadcast_to(
        jnp.sum(image_marks(), axis=1, keepdims=True), counts.shape
    )

    def count_copy(d):
        return remote(counts, counts_in.at[d], count_s.at[d], count_r.at[d], y_to[d])

    def pair(g):
        part = pl.ds(g * PER, PER)
        return remote(snd.at[part], prt.at[part], pair_s.at[g], pair_r.at[g], partner)

    def products(which, g, into):
        cols = pl.ds(pl.multiple_of(which * half + g * wide, wide), wide)
        part = pl.ds(g * PER, PER)
        fwd = dot(tokens[...], w_in[:, cols], 1, 0)
        into[part, 0] = fwd.reshape(PER, rows, wide).astype(into.dtype)
        bwd = dot(cotangent[...], w_out[cols, :], 1, 1)
        into[part, 1] = bwd.reshape(PER, rows, wide).astype(into.dtype)

    def onward(j):
        return remote(run.at[j], rcv.at[j], sum_s.at[j], sum_r.at[j], ahead)

    def back(j):
        spot = hid.at[core, j]
        return remote(spot, spot, back_s.at[j], back_r.at[j], behind)

    def side(j, which):
        spot = hid.at[which, j]
        return remote(spot, spot, side_s.at[j], side_r.at[j], partner)

    def save(j, which):
        return pltpu.make_async_copy(
            hid.at[which, j], hid_out.at[which, j], out_sem.at[which, j]
        )

    def begin(g):
        @pl.when(place == 0)
        def _():
            pair(g).wait_recv()

            @pl.loop(g * PER, (g + 1) * PER)
            def _(j):
                run[j] = (acc[j] + prt[j].astype(F32)).astype(BF16)
                onward(j).start()

    for load in loads[2:6]:
        load.wait()
    products(1 - core, 0, snd)
    pl.semaphore_wait(barrier, 5)
    pair(0).start()
    count_copy(0).start()
    count_copy(1).start()
    products(1 - core, 1, snd)
    pair(1).start()
    loads[6].wait()
    loads[7].wait()
    products(core, 0, acc)
    begin(0)
    products(core, 1, acc)
    begin(1)

    count_copy(0).wait_recv()
    count_copy(1).wait_recv()
    sizes = counts[...] + counts_in[0] + counts_in[1]
    sizes = jnp.concatenate([sizes, sizes], axis=1)
    per_token = dot(image_marks(), sizes, 0, 0)
    weight = jnp.where(
        per_token > 0.0, jnp.sqrt(IMAGE_MEAN / jnp.maximum(per_token, 1.0)), 0.0
    )
    weights[...] = weight
    span = weight.shape[1]
    for i in range(width // span):
        lanes = pl.ds(i * span, span)
        w_tok[:, lanes] = (tokens[:, lanes].astype(F32) * weight).astype(BF16)
        w_cot[:, lanes] = (cotangent[:, lanes].astype(F32) * weight).astype(BF16)
    keeps = [
        pltpu.make_async_copy(src, dst, w_sem.at[i])
        for i, (src, dst) in enumerate((
            (w_tok, w_tok_out), (w_cot, w_cot_out), (weights, weight_out),
        ))
    ]
    for copy in keeps:
        copy.start()

    def sum_step(j):
        own = acc[j] + prt[j].astype(F32)
        onward(j).wait_recv()
        run[j] = (own + rcv[j].astype(F32)).astype(BF16)
        onward(j).start()

    def finish_step(j):
        onward(j).wait_recv()
        pre = acc[j, 0] + prt[j, 0].astype(F32) + rcv[j, 0].astype(F32)
        grad = acc[j, 1] + prt[j, 1].astype(F32) + rcv[j, 1].astype(F32)
        act, slopes = gelu_parts(pre)
        hid[core, j, 0] = act.astype(BF16)
        hid[core, j, 1] = (grad * slopes).astype(BF16)
        back(j).start()
        side(j, core).start()
        save(j, core).start()

    def back_step(j, further):
        back(j).wait_recv()
        if further:
            back(j).start()
        side(j, core).start()
        save(j, core).start()

    def relay(lag):
        @pl.loop(0, lag)
        def _(j):
            sum_step(j)

        @pl.loop(lag, CHUNKS)
        def _(j):
            sum_step(j)
            back_step(j - lag, True)

        @pl.loop(CHUNKS - lag, CHUNKS)
        def _(j):
            back_step(j, True)

    @pl.when(place > 0)
    def _():
        for g in range(GROUPS):
            pair(g).wait_recv()

    @pl.when(place == 0)
    def _():
        @pl.loop(0, CHUNKS)
        def _(j):
            back_step(j, False)

    for spot, lag in ((1, 12), (2, 8)):
        @pl.when(place == spot)
        def _():
            relay(lag)

    @pl.when(place == 3)
    def _():
        @pl.loop(0, CHUNKS)
        def _(j):
            finish_step(j)

    @pl.loop(0, CHUNKS)
    def _(j):
        side(j, 1 - core).wait_recv()
        save(j, 1 - core).start()

    for g in range(GROUPS):
        pair(g).wait_send()
        count_copy(g).wait_send()
    for copy in keeps:
        copy.wait()

    @pl.loop(0, CHUNKS)
    def _(j):
        side(j, core).wait_send()
        save(j, 0).wait()
        save(j, 1).wait()

    @pl.when(place < 3)
    def _():
        @pl.loop(0, CHUNKS)
        def _(j):
            onward(j).wait_send()

    @pl.when(place > 0)
    def _():
        @pl.loop(0, CHUNKS)
        def _(j):
            back(j).wait_send()


def row_stage(mesh_shape, tokens, cotangent, w_in, w_out, seg, keep):
    toks, width = tokens.shape
    cols = w_in.shape[1]
    slab = (CHUNKS, 2, toks // PER, cols // 2 // GROUPS)
    dma = pltpu.SemaphoreType.DMA
    args = [
        pltpu.with_memory_space_constraint(x, pltpu.MemorySpace.HBM)
        for x in (tokens, cotangent, w_in, w_out, seg, keep)
    ]
    return pl.pallas_call(
        functools.partial(row_kernel, mesh_shape["batch"]),
        out_shape=(
            jax.ShapeDtypeStruct((2,) + slab, BF16),
            jax.ShapeDtypeStruct((toks, width), BF16),
            jax.ShapeDtypeStruct((toks, width), BF16),
            jax.ShapeDtypeStruct((toks, 256), F32),
        ),
        in_specs=[pl.BlockSpec(memory_space=pltpu.MemorySpace.HBM)] * 6,
        out_specs=(pl.BlockSpec(memory_space=pl.ANY),) * 4,
        scratch_shapes=[
            pltpu.VMEM((toks, width), BF16),
            pltpu.VMEM((toks, width), BF16),
            pltpu.VMEM((width, cols), BF16),
            pltpu.VMEM((cols, width), BF16),
            pltpu.VMEM((1, toks), jnp.int32),
            pltpu.VMEM((1, toks), jnp.int32),
            pltpu.VMEM(slab, BF16),
            pltpu.VMEM(slab, BF16),
            pltpu.VMEM(slab, F32),
            pltpu.VMEM(slab, BF16),
            pltpu.VMEM(slab, BF16),
            pltpu.VMEM((2,) + slab, BF16),
            pltpu.VMEM((toks, width), BF16),
            pltpu.VMEM((toks, width), BF16),
            pltpu.VMEM((toks, 256), F32),
            pltpu.VMEM((SEGS, 128), F32),
            pltpu.VMEM((2, SEGS, 128), F32),
            dma((GROUPS,)), dma((GROUPS,)),
            dma((CHUNKS,)), dma((CHUNKS,)),
            dma((CHUNKS,)), dma((CHUNKS,)),
            dma((CHUNKS,)), dma((CHUNKS,)),
            dma((2,)), dma((2,)),
            dma((2, CHUNKS)), dma((8,)), dma((3,)),
        ],
        compiler_params=pltpu.CompilerParams(
            collective_id=0, has_side_effects=True, vmem_limit_bytes=36 << 20
        ),
        cost_estimate=pl.CostEstimate(
            flops=4 * toks * width * cols, bytes_accessed=40 << 20, transcendentals=0
        ),
        name="row_stage",
    )(*args)


def grad_kernel(
    n_batch, n_x, n_z,
    hid, w_tok, w_cot, w_in, weights,
    g_tok, g_in, g_out,
    grads, y_first, y_rest, part, x_first, x_last, z_send, z_recv, total,
    y_s, y_r, x_s, x_r, z_s, z_r, zg_s, zg_r, xg_s, xg_r, out_sem,
):
    b = lax.axis_index("batch")
    col = lax.axis_index("col")
    xi = col // n_z
    q = col % n_z
    wide = hid.shape[4]
    toks = w_tok.shape[0]
    third = part.shape[2]
    piece = grads.shape[2]
    split = piece // 2
    own_rows = toks // n_x
    own_half = own_rows // 2
    own_split = own_half // 2

    y_next = {"batch": (b + 1) % n_batch}
    y_prev = {"batch": (b + n_batch - 1) % n_batch}
    x_next = {"col": ((xi + 1) % n_x) * n_z + q}
    x_prev = {"col": ((xi + n_x - 1) % n_x) * n_z + q}
    z_one = {"col": xi * n_z + (q + 1) % n_z}
    z_two = {"col": xi * n_z + (q + 2) % n_z}
    y_to = (y_next, y_prev)
    x_to = (x_next, x_prev)
    z_to = (z_one, z_two)

    barrier = pltpu.get_barrier_semaphore()
    for where in y_to + x_to + z_to:
        pl.semaphore_signal(barrier, inc=1, device_id=where, device_id_type=MESH)

    blocks = [(h, g) for h in range(2) for g in range(GROUPS)]

    def hidden(h, g, a):
        return hid[h, g * PER:(g + 1) * PER, a].reshape(toks, wide)

    def place(h, g):
        first = (h * GROUPS + g) * wide
        return slice(first, first + wide)

    def rows_of(ref, owner, start, size):
        first = pl.multiple_of(owner * own_rows + start, size)
        return ref.at[:, pl.ds(first, size), :]

    x_far = (xi + 2) % n_x
    x_near = ((xi + 1) % n_x, (xi + n_x - 1) % n_x)

    def x_sum(u, s, d):
        start = u * own_half
        if s == 0:
            src = rows_of(part, x_far, start + d * own_split, own_split)
            dst = x_first.at[u, d]
        else:
            src = rows_of(part, x_near[d], start, own_half)
            dst = x_last.at[u, d]
        return remote(src, dst, x_s.at[u, s, d], x_r.at[u, s, d], x_to[d])

    def y_owner(s, d):
        shift = 4 - s
        return (b + shift) % n_batch if d == 0 else (b + n_batch - shift) % n_batch

    def y_sum(a, s, d):
        src = grads.at[a, y_owner(s, d)]
        if s == 0:
            src = src.at[pl.ds(d * split, split), :]
            dst = y_first.at[a, d]
        else:
            dst = y_rest.at[a, d, s - 1]
        return remote(src, dst, y_s.at[a, s, d], y_r.at[a, s, d], y_to[d])

    def products(a, source):
        for h, g in blocks:
            block = dot(source[...], hidden(h, g, 1 - a), 0, 0)
            grads[a, :, :, place(h, g)] = block.reshape(n_batch, piece, wide).astype(BF16)

    def y_begin(a):
        y_sum(a, 0, 0).start()
        y_sum(a, 0, 1).start()

    def input_products():
        for i in range(3):
            rows = pl.ds(i * third, third)
            raw = sum(
                dot(hidden(h, g, 1), w_in[rows, place(h, g)], 1, 1) for h, g in blocks
            )
            part[i] = (raw * weights[...]).astype(BF16)
        for u in range(2):
            x_sum(u, 0, 0).start()
            x_sum(u, 0, 1).start()

    def y_onward(a, s):
        for d in range(2):
            y_sum(a, s - 1, d).wait_recv()
            owner = y_owner(s, d)
            if s == 1:
                lines = pl.ds(d * split, split)
                grads[a, owner, lines, :] = (
                    grads[a, owner, lines, :].astype(F32) + y_first[a, d].astype(F32)
                ).astype(BF16)
            else:
                grads[a, owner] = (
                    grads[a, owner].astype(F32) + y_rest[a, d, s - 2].astype(F32)
                ).astype(BF16)
            y_sum(a, s, d).start()

    def y_finish(a, out):
        y_sum(a, 3, 0).wait_recv()
        y_sum(a, 3, 1).wait_recv()
        out[...] = (
            grads[a, b].astype(F32)
            + y_rest[a, 0, 2].astype(F32)
            + y_rest[a, 1, 2].astype(F32)
        ).astype(BF16)

    def x_onward(u):
        for d in range(2):
            x_sum(u, 0, d).wait_recv()
            first = x_near[d] * own_rows + u * own_half + d * own_split
            lines = pl.ds(pl.multiple_of(first, own_split), own_split)
            part[:, lines, :] = (
                part[:, lines, :].astype(F32) + x_first[u, d].astype(F32)
            ).astype(BF16)
            x_sum(u, 1, d).start()

    def z_sum(u, k):
        target = (q + 1 + k) % n_z
        return remote(
            z_send.at[u, target], z_recv.at[u, k], z_s.at[u, k], z_r.at[u, k], z_to[k]
        )

    def mine(u):
        return pl.ds(pl.multiple_of(xi * own_rows + u * own_half, own_half), own_half)

    def z_scatter(u):
        x_sum(u, 1, 0).wait_recv()
        x_sum(u, 1, 1).wait_recv()
        z_send[u] = (
            part[:, mine(u), :].astype(F32)
            + x_last[u, 0].astype(F32)
            + x_last[u, 1].astype(F32)
        ).astype(BF16)
        z_sum(u, 0).start()
        z_sum(u, 1).start()

    def z_give(u, k):
        spot = total.at[q, mine(u), :]
        return remote(spot, spot, zg_s.at[u, k], zg_r.at[u, k], z_to[k])

    def z_gather(u):
        z_sum(u, 0).wait_recv()
        z_sum(u, 1).wait_recv()
        total[q, mine(u), :] = (
            z_send[u, q].astype(F32)
            + z_recv[u, 0].astype(F32)
            + z_recv[u, 1].astype(F32)
        ).astype(BF16)
        z_give(u, 0).start()
        z_give(u, 1).start()

    def x_give(u, s, d):
        start = u * own_half
        if s == 0:
            spot = rows_of(total, xi, start, own_half)
        else:
            spot = rows_of(total, x_near[1 - d], start + d * own_split, own_split)
        return remote(spot, spot, xg_s.at[u, s, d], xg_r.at[u, s, d], x_to[d])

    def x_gather(u):
        z_give(u, 0).wait_recv()
        z_give(u, 1).wait_recv()
        x_give(u, 0, 0).start()
        x_give(u, 0, 1).start()

    def x_forward(u):
        for d in range(2):
            x_give(u, 0, d).wait_recv()
            x_give(u, 1, d).start()

    def save(i):
        return pltpu.make_async_copy(
            total.at[i], g_tok.at[:, pl.ds(i * third, third)], out_sem.at[i]
        )

    products(1, w_cot)
    pl.semaphore_wait(barrier, 6)
    y_begin(1)
    input_products()
    products(0, w_tok)
    y_begin(0)
    x_onward(0)
    x_onward(1)
    z_scatter(0)
    y_onward(1, 1)
    z_scatter(1)
    y_onward(0, 1)
    z_gather(0)
    y_onward(1, 2)
    z_gather(1)
    y_onward(0, 2)
    x_gather(0)
    y_onward(1, 3)
    x_gather(1)
    x_forward(0)
    y_onward(0, 3)
    x_forward(1)
    y_finish(1, g_out)
    for u in range(2):
        x_give(u, 1, 0).wait_recv()
        x_give(u, 1, 1).wait_recv()
    for i in range(3):
        save(i).start()
    y_finish(0, g_in)

    for d in range(2):
        for u in range(2):
            z_sum(u, d).wait_send()
            z_give(u, d).wait_send()
            for s in range(2):
                x_sum(u, s, d).wait_send()
                x_give(u, s, d).wait_send()
        for s in range(4):
            for a in range(2):
                y_sum(a, s, d).wait_send()
    for i in range(3):
        save(i).wait()


def grad_stage(mesh_shape, hid, w_tok, w_cot, w_in, weights):
    n_batch = mesh_shape["batch"]
    n_x, n_z = 4, mesh_shape["col"] // 4
    toks, width = w_tok.shape
    cols = w_in.shape[1]
    third = width // 3
    piece = width // n_batch
    own = toks // n_x
    dma = pltpu.SemaphoreType.DMA
    vmem = pl.BlockSpec(memory_space=pltpu.VMEM)
    return pl.pallas_call(
        functools.partial(grad_kernel, n_batch, n_x, n_z),
        out_shape=(
            jax.ShapeDtypeStruct((toks, width), BF16),
            jax.ShapeDtypeStruct((piece, cols), BF16),
            jax.ShapeDtypeStruct((piece, cols), BF16),
        ),
        in_specs=[vmem] * 5,
        out_specs=(pl.BlockSpec(memory_space=pl.ANY), vmem, vmem),
        scratch_shapes=[
            pltpu.VMEM((2, n_batch, piece, cols), BF16),
            pltpu.VMEM((2, 2, piece // 2, cols), BF16),
            pltpu.VMEM((2, 2, 3, piece, cols), BF16),
            pltpu.VMEM((3, toks, third), BF16),
            pltpu.VMEM((2, 2, 3, own // 4, third), BF16),
            pltpu.VMEM((2, 2, 3, own // 2, third), BF16),
            pltpu.VMEM((2, 3, own // 2, third), BF16),
            pltpu.VMEM((2, 2, own // 2, third), BF16),
            pltpu.VMEM((3, toks, third), BF16),
            dma((2, 4, 2)), dma((2, 4, 2)),
            dma((2, 2, 2)), dma((2, 2, 2)),
            dma((2, 2)), dma((2, 2)),
            dma((2, 2)), dma((2, 2)),
            dma((2, 2, 2)), dma((2, 2, 2)),
            dma((3,)),
        ],
        compiler_params=pltpu.CompilerParams(
            collective_id=1, has_side_effects=True, vmem_limit_bytes=36 << 20
        ),
        cost_estimate=pl.CostEstimate(
            flops=6 * toks * width * cols, bytes_accessed=40 << 20, transcendentals=0
        ),
        name="grad_stage",
    )(hid, w_tok, w_cot, w_in, weights)


def publish_kernel(*refs):
    count = (len(refs) - 1) // 2
    copies = [
        pltpu.make_async_copy(refs[i], refs[count + i], refs[-1].at[i])
        for i in range(count)
    ]
    for copy in copies:
        copy.start()
    for copy in copies:
        copy.wait()


def publish(*arrays):
    anywhere = pl.BlockSpec(memory_space=pl.ANY)
    return pl.pallas_call(
        publish_kernel,
        out_shape=tuple(jax.ShapeDtypeStruct(x.shape, x.dtype) for x in arrays),
        in_specs=[anywhere] * len(arrays),
        out_specs=(anywhere,) * len(arrays),
        scratch_shapes=[pltpu.SemaphoreType.DMA((len(arrays),))],
        compiler_params=pltpu.CompilerParams(vmem_limit_bytes=8 << 20),
        name="publish",
    )(*arrays)


def per_device(mesh_shape, tokens, cotangent, weight_in, weight_out, segment_ids, keep_mask):
    hid, w_tok, w_cot, weights = row_stage(
        mesh_shape, tokens, cotangent, weight_in, weight_out,
        segment_ids[None, :], keep_mask[None, :],
    )
    grad_tokens, grad_in, grad_out = publish(
        *grad_stage(mesh_shape, hid, w_tok, w_cot, weight_in, weights)
    )
    return (grad_tokens, grad_in, grad_out.T)


def solution(mesh):
    return jax.shard_map(
        functools.partial(per_device, dict(mesh.shape)),
        mesh=mesh,
        in_specs=(
            P("batch", "row"),
            P("batch", "row"),
            P("row", "col"),
            P("col", "row"),
            P("batch"),
            P("batch"),
        ),
        out_specs=(P("batch", "row"), P(("row", "batch"), "col"), P("col", ("row", "batch"))),
        check_vma=False,
    )
```

```python
import functools

import jax
import jax.numpy as jnp
from jax import lax
from jax.experimental import pallas as pl
from jax.experimental.pallas import tpu as pltpu
from jax.sharding import PartitionSpec as P

SEGS = 32
IMAGE_MEAN = 128.0
MESH = pl.DeviceIdType.MESH

inv_root_two = 0.7071067811865476
inv_root_tau = 0.3989422804014327

F32 = jnp.float32
BF16 = jnp.bfloat16


def dot(left, right, lc, rc):
    return lax.dot_general(
        left, right, (((lc,), (rc,)), ((), ())), preferred_element_type=F32
    )


def gelu_parts(pre_act):
    normal_cdf = 0.5 * (1.0 + lax.erf(pre_act * inv_root_two))
    slopes = normal_cdf + pre_act * jnp.exp(-0.5 * pre_act * pre_act) * inv_root_tau
    return (pre_act * normal_cdf, slopes)


def remote(src, dst, send, recv, where):
    return pltpu.make_async_remote_copy(
        src_ref=src,
        dst_ref=dst,
        send_sem=send,
        recv_sem=recv,
        device_id=where,
        device_id_type=MESH,
    )


GROUPS = 2
PER = 8
CHUNKS = GROUPS * PER


def row_kernel(
    n_batch,
    tokens_h, cotangent_h, w_in_h, w_out_h, seg_h, keep_h,
    hid_out, w_tok_out, w_cot_out, weight_out,
    tokens, cotangent, w_in, w_out, seg, keep,
    snd, prt, acc, rcv, run, hid,
    w_tok, w_cot, weights, counts, counts_in,
    pair_s, pair_r, sum_s, sum_r, back_s, back_r, side_s, side_r,
    count_s, count_r, out_sem, in_sem, w_sem,
):
    b = lax.axis_index("batch")
    row = lax.axis_index("row")
    core = row % 2
    z = row // 2
    place = core * z + (1 - core) * (3 - z)
    step = 4 * core - 2
    ahead = {"row": (row + step + 8) % 8}
    behind = {"row": (row - step + 8) % 8}
    partner = {"row": row + 1 - 2 * core}
    y_to = ({"batch": (b + 1) % n_batch}, {"batch": (b + n_batch - 1) % n_batch})
    rows, wide = acc.shape[2], acc.shape[3]
    toks, width = tokens.shape
    half = GROUPS * wide

    barrier = pltpu.get_barrier_semaphore()
    for where in (partner, ahead, behind) + y_to:
        pl.semaphore_signal(barrier, inc=1, device_id=where, device_id_type=MESH)

    def columns(which):
        return pl.ds(pl.multiple_of(which * half, half), half)

    other = columns(1 - core)
    mine = columns(core)
    loads = [
        pltpu.make_async_copy(src, dst, in_sem.at[i])
        for i, (src, dst) in enumerate((
            (seg_h, seg),
            (keep_h, keep),
            (tokens_h, tokens),
            (w_in_h.at[:, other], w_in.at[:, other]),
            (cotangent_h, cotangent),
            (w_out_h.at[other, :], w_out.at[other, :]),
            (w_in_h.at[:, mine], w_in.at[:, mine]),
            (w_out_h.at[mine, :], w_out.at[mine, :]),
        ))
    ]
    for load in loads:
        load.start()

    loads[0].wait()
    loads[1].wait()
    labels = lax.broadcasted_iota(jnp.int32, (SEGS, toks), 0)

    def image_marks():
        return jnp.where((labels == seg[...]) & (keep[...] == 1), 1.0, 0.0).astype(F32)

    counts[...] = jnp.broadcast_to(
        jnp.sum(image_marks(), axis=1, keepdims=True), counts.shape
    )

    def count_copy(d):
        return remote(counts, counts_in.at[d], count_s.at[d], count_r.at[d], y_to[d])

    def pair(g):
        part = pl.ds(g * PER, PER)
        return remote(snd.at[part], prt.at[part], pair_s.at[g], pair_r.at[g], partner)

    def products(which, g, into):
        cols = pl.ds(pl.multiple_of(which * half + g * wide, wide), wide)
        part = pl.ds(g * PER, PER)
        fwd = dot(tokens[...], w_in[:, cols], 1, 0)
        into[part, 0] = fwd.reshape(PER, rows, wide).astype(into.dtype)
        bwd = dot(cotangent[...], w_out[cols, :], 1, 1)
        into[part, 1] = bwd.reshape(PER, rows, wide).astype(into.dtype)

    def onward(j):
        return remote(run.at[j], rcv.at[j], sum_s.at[j], sum_r.at[j], ahead)

    def back(j):
        spot = hid.at[core, j]
        return remote(spot, spot, back_s.at[j], back_r.at[j], behind)

    def side(j, which):
        spot = hid.at[which, j]
        return remote(spot, spot, side_s.at[j], side_r.at[j], partner)

    def save(j, which):
        return pltpu.make_async_copy(
            hid.at[which, j], hid_out.at[which, j], out_sem.at[which, j]
        )

    def begin(g):
        @pl.when(place == 0)
        def _():
            pair(g).wait_recv()

            @pl.loop(g * PER, (g + 1) * PER)
            def _(j):
                run[j] = (acc[j] + prt[j].astype(F32)).astype(BF16)
                onward(j).start()

    for load in loads[2:6]:
        load.wait()
    products(1 - core, 0, snd)
    pl.semaphore_wait(barrier, 5)
    pair(0).start()
    count_copy(0).start()
    count_copy(1).start()
    products(1 - core, 1, snd)
    pair(1).start()
    loads[6].wait()
    loads[7].wait()
    products(core, 0, acc)
    begin(0)
    products(core, 1, acc)
    begin(1)

    count_copy(0).wait_recv()
    count_copy(1).wait_recv()
    sizes = counts[...] + counts_in[0] + counts_in[1]
    sizes = jnp.concatenate([sizes, sizes], axis=1)
    per_token = dot(image_marks(), sizes, 0, 0)
    weight = jnp.where(
        per_token > 0.0, jnp.sqrt(IMAGE_MEAN / jnp.maximum(per_token, 1.0)), 0.0
    )
    weights[...] = weight
    span = weight.shape[1]
    for i in range(width // span):
        lanes = pl.ds(i * span, span)
        w_tok[:, lanes] = (tokens[:, lanes].astype(F32) * weight).astype(BF16)
        w_cot[:, lanes] = (cotangent[:, lanes].astype(F32) * weight).astype(BF16)
    keeps = [
        pltpu.make_async_copy(src, dst, w_sem.at[i])
        for i, (src, dst) in enumerate((
            (w_tok, w_tok_out), (w_cot, w_cot_out), (weights, weight_out),
        ))
    ]
    for copy in keeps:
        copy.start()

    def sum_step(j):
        own = acc[j] + prt[j].astype(F32)
        onward(j).wait_recv()
        run[j] = (own + rcv[j].astype(F32)).astype(BF16)
        onward(j).start()

    def finish_step(j):
        onward(j).wait_recv()
        pre = acc[j, 0] + prt[j, 0].astype(F32) + rcv[j, 0].astype(F32)
        grad = acc[j, 1] + prt[j, 1].astype(F32) + rcv[j, 1].astype(F32)
        act, slopes = gelu_parts(pre)
        hid[core, j, 0] = act.astype(BF16)
        hid[core, j, 1] = (grad * slopes).astype(BF16)
        back(j).start()
        side(j, core).start()
        save(j, core).start()

    def back_step(j, further):
        back(j).wait_recv()
        if further:
            back(j).start()
        side(j, core).start()
        save(j, core).start()

    def relay(lag):
        @pl.loop(0, lag)
        def _(j):
            sum_step(j)

        @pl.loop(lag, CHUNKS)
        def _(j):
            sum_step(j)
            back_step(j - lag, True)

        @pl.loop(CHUNKS - lag, CHUNKS)
        def _(j):
            back_step(j, True)

    @pl.when(place > 0)
    def _():
        for g in range(GROUPS):
            pair(g).wait_recv()

    @pl.when(place == 0)
    def _():
        @pl.loop(0, CHUNKS)
        def _(j):
            back_step(j, False)

    for spot, lag in ((1, 15), (2, 10)):
        @pl.when(place == spot)
        def _():
            relay(lag)

    @pl.when(place == 3)
    def _():
        @pl.loop(0, CHUNKS)
        def _(j):
            finish_step(j)

    @pl.loop(0, CHUNKS)
    def _(j):
        side(j, 1 - core).wait_recv()
        save(j, 1 - core).start()

    for g in range(GROUPS):
        pair(g).wait_send()
        count_copy(g).wait_send()
    for copy in keeps:
        copy.wait()

    @pl.loop(0, CHUNKS)
    def _(j):
        side(j, core).wait_send()
        save(j, 0).wait()
        save(j, 1).wait()

    @pl.when(place < 3)
    def _():
        @pl.loop(0, CHUNKS)
        def _(j):
            onward(j).wait_send()

    @pl.when(place > 0)
    def _():
        @pl.loop(0, CHUNKS)
        def _(j):
            back(j).wait_send()


def row_stage(mesh_shape, tokens, cotangent, w_in, w_out, seg, keep):
    toks, width = tokens.shape
    cols = w_in.shape[1]
    slab = (CHUNKS, 2, toks // PER, cols // 2 // GROUPS)
    dma = pltpu.SemaphoreType.DMA
    args = [
        pltpu.with_memory_space_constraint(x, pltpu.MemorySpace.HBM)
        for x in (tokens, cotangent, w_in, w_out, seg, keep)
    ]
    return pl.pallas_call(
        functools.partial(row_kernel, mesh_shape["batch"]),
        out_shape=(
            jax.ShapeDtypeStruct((2,) + slab, BF16),
            jax.ShapeDtypeStruct((toks, width), BF16),
            jax.ShapeDtypeStruct((toks, width), BF16),
            jax.ShapeDtypeStruct((toks, 256), F32),
        ),
        in_specs=[pl.BlockSpec(memory_space=pltpu.MemorySpace.HBM)] * 6,
        out_specs=(pl.BlockSpec(memory_space=pl.ANY),) * 4,
        scratch_shapes=[
            pltpu.VMEM((toks, width), BF16),
            pltpu.VMEM((toks, width), BF16),
            pltpu.VMEM((width, cols), BF16),
            pltpu.VMEM((cols, width), BF16),
            pltpu.VMEM((1, toks), jnp.int32),
            pltpu.VMEM((1, toks), jnp.int32),
            pltpu.VMEM(slab, BF16),
            pltpu.VMEM(slab, BF16),
            pltpu.VMEM(slab, F32),
            pltpu.VMEM(slab, BF16),
            pltpu.VMEM(slab, BF16),
            pltpu.VMEM((2,) + slab, BF16),
            pltpu.VMEM((toks, width), BF16),
            pltpu.VMEM((toks, width), BF16),
            pltpu.VMEM((toks, 256), F32),
            pltpu.VMEM((SEGS, 128), F32),
            pltpu.VMEM((2, SEGS, 128), F32),
            dma((GROUPS,)), dma((GROUPS,)),
            dma((CHUNKS,)), dma((CHUNKS,)),
            dma((CHUNKS,)), dma((CHUNKS,)),
            dma((CHUNKS,)), dma((CHUNKS,)),
            dma((2,)), dma((2,)),
            dma((2, CHUNKS)), dma((8,)), dma((3,)),
        ],
        compiler_params=pltpu.CompilerParams(
            collective_id=0, has_side_effects=True, vmem_limit_bytes=36 << 20
        ),
        cost_estimate=pl.CostEstimate(
            flops=4 * toks * width * cols, bytes_accessed=40 << 20, transcendentals=0
        ),
        name="row_stage",
    )(*args)


def grad_kernel(
    n_batch, n_x, n_z,
    hid, w_tok, w_cot, w_in, weights,
    g_tok, g_in, g_out,
    grads, y_first, y_rest, part, x_first, x_last, z_send, z_recv, total,
    y_s, y_r, x_s, x_r, z_s, z_r, zg_s, zg_r, xg_s, xg_r, out_sem,
):
    b = lax.axis_index("batch")
    col = lax.axis_index("col")
    xi = col // n_z
    q = col % n_z
    wide = hid.shape[4]
    toks = w_tok.shape[0]
    third = part.shape[2]
    piece = grads.shape[2]
    split = piece // 2
    own_rows = toks // n_x
    own_half = own_rows // 2
    own_split = own_half // 2

    y_next = {"batch": (b + 1) % n_batch}
    y_prev = {"batch": (b + n_batch - 1) % n_batch}
    x_next = {"col": ((xi + 1) % n_x) * n_z + q}
    x_prev = {"col": ((xi + n_x - 1) % n_x) * n_z + q}
    z_one = {"col": xi * n_z + (q + 1) % n_z}
    z_two = {"col": xi * n_z + (q + 2) % n_z}
    y_to = (y_next, y_prev)
    x_to = (x_next, x_prev)
    z_to = (z_one, z_two)

    barrier = pltpu.get_barrier_semaphore()
    for where in y_to + x_to + z_to:
        pl.semaphore_signal(barrier, inc=1, device_id=where, device_id_type=MESH)

    blocks = [(h, g) for h in range(2) for g in range(GROUPS)]

    def hidden(h, g, a):
        return hid[h, g * PER:(g + 1) * PER, a].reshape(toks, wide)

    def place(h, g):
        first = (h * GROUPS + g) * wide
        return slice(first, first + wide)

    def rows_of(ref, owner, start, size):
        first = pl.multiple_of(owner * own_rows + start, size)
        return ref.at[:, pl.ds(first, size), :]

    x_far = (xi + 2) % n_x
    x_near = ((xi + 1) % n_x, (xi + n_x - 1) % n_x)

    def x_sum(u, s, d):
        start = u * own_half
        if s == 0:
            src = rows_of(part, x_far, start + d * own_split, own_split)
            dst = x_first.at[u, d]
        else:
            src = rows_of(part, x_near[d], start, own_half)
            dst = x_last.at[u, d]
        return remote(src, dst, x_s.at[u, s, d], x_r.at[u, s, d], x_to[d])

    def y_owner(s, d):
        shift = 4 - s
        return (b + shift) % n_batch if d == 0 else (b + n_batch - shift) % n_batch

    def y_sum(a, s, d):
        src = grads.at[a, y_owner(s, d)]
        if s == 0:
            src = src.at[pl.ds(d * split, split), :]
            dst = y_first.at[a, d]
        else:
            dst = y_rest.at[a, d, s - 1]
        return remote(src, dst, y_s.at[a, s, d], y_r.at[a, s, d], y_to[d])

    def products(a, source):
        for h, g in blocks:
            block = dot(source[...], hidden(h, g, 1 - a), 0, 0)
            grads[a, :, :, place(h, g)] = block.reshape(n_batch, piece, wide).astype(BF16)

    def y_begin(a):
        y_sum(a, 0, 0).start()
        y_sum(a, 0, 1).start()

    def input_products():
        for i in range(3):
            rows = pl.ds(i * third, third)
            raw = sum(
                dot(hidden(h, g, 1), w_in[rows, place(h, g)], 1, 1) for h, g in blocks
            )
            part[i] = (raw * weights[...]).astype(BF16)

    def x_begin():
        for u in range(2):
            x_sum(u, 0, 0).start()
            x_sum(u, 0, 1).start()

    def y_onward(a, s):
        for d in range(2):
            y_sum(a, s - 1, d).wait_recv()
            owner = y_owner(s, d)
            if s == 1:
                lines = pl.ds(d * split, split)
                grads[a, owner, lines, :] = (
                    grads[a, owner, lines, :].astype(F32) + y_first[a, d].astype(F32)
                ).astype(BF16)
            else:
                grads[a, owner] = (
                    grads[a, owner].astype(F32) + y_rest[a, d, s - 2].astype(F32)
                ).astype(BF16)
            y_sum(a, s, d).start()

    def y_finish(a, out):
        y_sum(a, 3, 0).wait_recv()
        y_sum(a, 3, 1).wait_recv()
        out[...] = (
            grads[a, b].astype(F32)
            + y_rest[a, 0, 2].astype(F32)
            + y_rest[a, 1, 2].astype(F32)
        ).astype(BF16)

    def x_onward(u):
        for d in range(2):
            x_sum(u, 0, d).wait_recv()
            first = x_near[d] * own_rows + u * own_half + d * own_split
            lines = pl.ds(pl.multiple_of(first, own_split), own_split)
            part[:, lines, :] = (
                part[:, lines, :].astype(F32) + x_first[u, d].astype(F32)
            ).astype(BF16)
            x_sum(u, 1, d).start()

    def z_sum(u, k):
        target = (q + 1 + k) % n_z
        return remote(
            z_send.at[u, target], z_recv.at[u, k], z_s.at[u, k], z_r.at[u, k], z_to[k]
        )

    def mine(u):
        return pl.ds(pl.multiple_of(xi * own_rows + u * own_half, own_half), own_half)

    def z_scatter(u):
        x_sum(u, 1, 0).wait_recv()
        x_sum(u, 1, 1).wait_recv()
        z_send[u] = (
            part[:, mine(u), :].astype(F32)
            + x_last[u, 0].astype(F32)
            + x_last[u, 1].astype(F32)
        ).astype(BF16)
        z_sum(u, 0).start()
        z_sum(u, 1).start()

    def z_give(u, k):
        spot = total.at[q, mine(u), :]
        return remote(spot, spot, zg_s.at[u, k], zg_r.at[u, k], z_to[k])

    def z_gather(u):
        z_sum(u, 0).wait_recv()
        z_sum(u, 1).wait_recv()
        total[q, mine(u), :] = (
            z_send[u, q].astype(F32)
            + z_recv[u, 0].astype(F32)
            + z_recv[u, 1].astype(F32)
        ).astype(BF16)
        z_give(u, 0).start()
        z_give(u, 1).start()

    def x_give(u, s, d):
        start = u * own_half
        if s == 0:
            spot = rows_of(total, xi, start, own_half)
        else:
            spot = rows_of(total, x_near[1 - d], start + d * own_split, own_split)
        return remote(spot, spot, xg_s.at[u, s, d], xg_r.at[u, s, d], x_to[d])

    def x_gather(u):
        z_give(u, 0).wait_recv()
        z_give(u, 1).wait_recv()
        x_give(u, 0, 0).start()
        x_give(u, 0, 1).start()

    def x_forward(u):
        for d in range(2):
            x_give(u, 0, d).wait_recv()
            x_give(u, 1, d).start()

    def save(i):
        return pltpu.make_async_copy(
            total.at[i], g_tok.at[:, pl.ds(i * third, third)], out_sem.at[i]
        )

    input_products()
    pl.semaphore_wait(barrier, 6)
    x_begin()
    products(0, w_tok)
    y_begin(0)
    products(1, w_cot)
    y_begin(1)
    x_onward(0)
    x_onward(1)
    y_onward(0, 1)
    z_scatter(0)
    y_onward(1, 1)
    z_scatter(1)
    y_onward(0, 2)
    z_gather(0)
    y_onward(1, 2)
    z_gather(1)
    y_onward(0, 3)
    x_gather(0)
    y_onward(1, 3)
    x_gather(1)
    x_forward(0)
    x_forward(1)
    y_finish(0, g_in)
    y_finish(1, g_out)
    for u in range(2):
        x_give(u, 1, 0).wait_recv()
        x_give(u, 1, 1).wait_recv()
    for i in range(3):
        save(i).start()

    for d in range(2):
        for u in range(2):
            z_sum(u, d).wait_send()
            z_give(u, d).wait_send()
            for s in range(2):
                x_sum(u, s, d).wait_send()
                x_give(u, s, d).wait_send()
        for s in range(4):
            for a in range(2):
                y_sum(a, s, d).wait_send()
    for i in range(3):
        save(i).wait()


def grad_stage(mesh_shape, hid, w_tok, w_cot, w_in, weights):
    n_batch = mesh_shape["batch"]
    n_x, n_z = 4, mesh_shape["col"] // 4
    toks, width = w_tok.shape
    cols = w_in.shape[1]
    third = width // 3
    piece = width // n_batch
    own = toks // n_x
    dma = pltpu.SemaphoreType.DMA
    vmem = pl.BlockSpec(memory_space=pltpu.VMEM)
    return pl.pallas_call(
        functools.partial(grad_kernel, n_batch, n_x, n_z),
        out_shape=(
            jax.ShapeDtypeStruct((toks, width), BF16),
            jax.ShapeDtypeStruct((piece, cols), BF16),
            jax.ShapeDtypeStruct((piece, cols), BF16),
        ),
        in_specs=[vmem] * 5,
        out_specs=(pl.BlockSpec(memory_space=pl.ANY), vmem, vmem),
        scratch_shapes=[
            pltpu.VMEM((2, n_batch, piece, cols), BF16),
            pltpu.VMEM((2, 2, piece // 2, cols), BF16),
            pltpu.VMEM((2, 2, 3, piece, cols), BF16),
            pltpu.VMEM((3, toks, third), BF16),
            pltpu.VMEM((2, 2, 3, own // 4, third), BF16),
            pltpu.VMEM((2, 2, 3, own // 2, third), BF16),
            pltpu.VMEM((2, 3, own // 2, third), BF16),
            pltpu.VMEM((2, 2, own // 2, third), BF16),
            pltpu.VMEM((3, toks, third), BF16),
            dma((2, 4, 2)), dma((2, 4, 2)),
            dma((2, 2, 2)), dma((2, 2, 2)),
            dma((2, 2)), dma((2, 2)),
            dma((2, 2)), dma((2, 2)),
            dma((2, 2, 2)), dma((2, 2, 2)),
            dma((3,)),
        ],
        compiler_params=pltpu.CompilerParams(
            collective_id=1, has_side_effects=True, vmem_limit_bytes=36 << 20
        ),
        cost_estimate=pl.CostEstimate(
            flops=6 * toks * width * cols, bytes_accessed=40 << 20, transcendentals=0
        ),
        name="grad_stage",
    )(hid, w_tok, w_cot, w_in, weights)


def publish_kernel(*refs):
    count = (len(refs) - 1) // 2
    copies = [
        pltpu.make_async_copy(refs[i], refs[count + i], refs[-1].at[i])
        for i in range(count)
    ]
    for copy in copies:
        copy.start()
    for copy in copies:
        copy.wait()


def publish(*arrays):
    anywhere = pl.BlockSpec(memory_space=pl.ANY)
    return pl.pallas_call(
        publish_kernel,
        out_shape=tuple(jax.ShapeDtypeStruct(x.shape, x.dtype) for x in arrays),
        in_specs=[anywhere] * len(arrays),
        out_specs=(anywhere,) * len(arrays),
        scratch_shapes=[pltpu.SemaphoreType.DMA((len(arrays),))],
        compiler_params=pltpu.CompilerParams(vmem_limit_bytes=8 << 20),
        name="publish",
    )(*arrays)


def per_device(mesh_shape, tokens, cotangent, weight_in, weight_out, segment_ids, keep_mask):
    hid, w_tok, w_cot, weights = row_stage(
        mesh_shape, tokens, cotangent, weight_in, weight_out,
        segment_ids[None, :], keep_mask[None, :],
    )
    grad_tokens, grad_in, grad_out = publish(
        *grad_stage(mesh_shape, hid, w_tok, w_cot, weight_in, weights)
    )
    return (grad_tokens, grad_in, grad_out.T)


def solution(mesh):
    return jax.shard_map(
        functools.partial(per_device, dict(mesh.shape)),
        mesh=mesh,
        in_specs=(
            P("batch", "row"),
            P("batch", "row"),
            P("row", "col"),
            P("col", "row"),
            P("batch"),
            P("batch"),
        ),
        out_specs=(P("batch", "row"), P(("row", "batch"), "col"), P("col", ("row", "batch"))),
        check_vma=False,
    )
```

```python
import functools

import jax
import jax.numpy as jnp
from jax import lax
from jax.experimental import pallas as pl
from jax.experimental.pallas import tpu as pltpu
from jax.sharding import PartitionSpec as P

SEGS = 32
IMAGE_MEAN = 128.0
MESH = pl.DeviceIdType.MESH

inv_root_two = 0.7071067811865476
inv_root_tau = 0.3989422804014327

F32 = jnp.float32
BF16 = jnp.bfloat16


def dot(left, right, lc, rc):
    return lax.dot_general(
        left, right, (((lc,), (rc,)), ((), ())), preferred_element_type=F32
    )


def gelu_parts(pre_act):
    normal_cdf = 0.5 * (1.0 + lax.erf(pre_act * inv_root_two))
    slopes = normal_cdf + pre_act * jnp.exp(-0.5 * pre_act * pre_act) * inv_root_tau
    return (pre_act * normal_cdf, slopes)


def remote(src, dst, send, recv, where):
    return pltpu.make_async_remote_copy(
        src_ref=src,
        dst_ref=dst,
        send_sem=send,
        recv_sem=recv,
        device_id=where,
        device_id_type=MESH,
    )


GROUPS = 2
PER = 8
CHUNKS = GROUPS * PER


def row_kernel(
    n_batch,
    tokens_h, cotangent_h, w_in_h, w_out_h, seg_h, keep_h,
    hid_out, w_tok_out, w_cot_out, weight_out,
    tokens, cotangent, w_in, w_out, seg, keep,
    snd, prt, acc, rcv, run, hid,
    w_tok, w_cot, weights, counts, counts_in,
    pair_s, pair_r, sum_s, sum_r, back_s, back_r, side_s, side_r,
    count_s, count_r, out_sem, in_sem, w_sem,
):
    b = lax.axis_index("batch")
    row = lax.axis_index("row")
    core = row % 2
    z = row // 2
    place = core * z + (1 - core) * (3 - z)
    step = 4 * core - 2
    ahead = {"row": (row + step + 8) % 8}
    behind = {"row": (row - step + 8) % 8}
    partner = {"row": row + 1 - 2 * core}
    y_to = ({"batch": (b + 1) % n_batch}, {"batch": (b + n_batch - 1) % n_batch})
    rows, wide = acc.shape[2], acc.shape[3]
    toks, width = tokens.shape
    half = GROUPS * wide

    barrier = pltpu.get_barrier_semaphore()
    for where in (partner, ahead, behind) + y_to:
        pl.semaphore_signal(barrier, inc=1, device_id=where, device_id_type=MESH)

    def columns(which):
        return pl.ds(pl.multiple_of(which * half, half), half)

    other = columns(1 - core)
    mine = columns(core)
    loads = [
        pltpu.make_async_copy(src, dst, in_sem.at[i])
        for i, (src, dst) in enumerate((
            (seg_h, seg),
            (keep_h, keep),
            (tokens_h, tokens),
            (w_in_h.at[:, other], w_in.at[:, other]),
            (cotangent_h, cotangent),
            (w_out_h.at[other, :], w_out.at[other, :]),
            (w_in_h.at[:, mine], w_in.at[:, mine]),
            (w_out_h.at[mine, :], w_out.at[mine, :]),
        ))
    ]
    for load in loads:
        load.start()

    loads[0].wait()
    loads[1].wait()
    labels = lax.broadcasted_iota(jnp.int32, (SEGS, toks), 0)

    def image_marks():
        return jnp.where((labels == seg[...]) & (keep[...] == 1), 1.0, 0.0).astype(F32)

    counts[...] = jnp.broadcast_to(
        jnp.sum(image_marks(), axis=1, keepdims=True), counts.shape
    )

    def count_copy(d):
        return remote(counts, counts_in.at[d], count_s.at[d], count_r.at[d], y_to[d])

    def pair(g):
        part = pl.ds(g * PER, PER)
        return remote(snd.at[part], prt.at[part], pair_s.at[g], pair_r.at[g], partner)

    def products(which, g, into):
        cols = pl.ds(pl.multiple_of(which * half + g * wide, wide), wide)
        part = pl.ds(g * PER, PER)
        fwd = dot(tokens[...], w_in[:, cols], 1, 0)
        into[part, 0] = fwd.reshape(PER, rows, wide).astype(into.dtype)
        bwd = dot(cotangent[...], w_out[cols, :], 1, 1)
        into[part, 1] = bwd.reshape(PER, rows, wide).astype(into.dtype)

    def onward(j):
        return remote(run.at[j], rcv.at[j], sum_s.at[j], sum_r.at[j], ahead)

    def back(j):
        spot = hid.at[core, j]
        return remote(spot, spot, back_s.at[j], back_r.at[j], behind)

    def side(j, which):
        spot = hid.at[which, j]
        return remote(spot, spot, side_s.at[j], side_r.at[j], partner)

    def save(j, which):
        return pltpu.make_async_copy(
            hid.at[which, j], hid_out.at[which, j], out_sem.at[which, j]
        )

    def begin(g):
        @pl.when(place == 0)
        def _():
            pair(g).wait_recv()

            @pl.loop(g * PER, (g + 1) * PER)
            def _(j):
                run[j] = (acc[j] + prt[j].astype(F32)).astype(BF16)
                onward(j).start()

    for load in loads[2:6]:
        load.wait()
    products(1 - core, 0, snd)
    pl.semaphore_wait(barrier, 5)
    pair(0).start()
    count_copy(0).start()
    count_copy(1).start()
    products(1 - core, 1, snd)
    pair(1).start()
    loads[6].wait()
    loads[7].wait()
    products(core, 0, acc)
    begin(0)
    products(core, 1, acc)
    begin(1)

    count_copy(0).wait_recv()
    count_copy(1).wait_recv()
    sizes = counts[...] + counts_in[0] + counts_in[1]
    sizes = jnp.concatenate([sizes, sizes], axis=1)
    per_token = dot(image_marks(), sizes, 0, 0)
    weight = jnp.where(
        per_token > 0.0, jnp.sqrt(IMAGE_MEAN / jnp.maximum(per_token, 1.0)), 0.0
    )
    weights[...] = weight
    span = weight.shape[1]
    for i in range(width // span):
        lanes = pl.ds(i * span, span)
        w_tok[:, lanes] = (tokens[:, lanes].astype(F32) * weight).astype(BF16)
        w_cot[:, lanes] = (cotangent[:, lanes].astype(F32) * weight).astype(BF16)
    keeps = [
        pltpu.make_async_copy(src, dst, w_sem.at[i])
        for i, (src, dst) in enumerate((
            (w_tok, w_tok_out), (w_cot, w_cot_out), (weights, weight_out),
        ))
    ]
    for copy in keeps:
        copy.start()

    def sum_step(j):
        own = acc[j] + prt[j].astype(F32)
        onward(j).wait_recv()
        run[j] = (own + rcv[j].astype(F32)).astype(BF16)
        onward(j).start()

    def finish_step(j):
        onward(j).wait_recv()
        pre = acc[j, 0] + prt[j, 0].astype(F32) + rcv[j, 0].astype(F32)
        grad = acc[j, 1] + prt[j, 1].astype(F32) + rcv[j, 1].astype(F32)
        act, slopes = gelu_parts(pre)
        hid[core, j, 0] = act.astype(BF16)
        hid[core, j, 1] = (grad * slopes).astype(BF16)
        back(j).start()
        side(j, core).start()
        save(j, core).start()

    def back_step(j, further):
        back(j).wait_recv()
        if further:
            back(j).start()
        side(j, core).start()
        save(j, core).start()

    def relay(lag):
        @pl.loop(0, lag)
        def _(j):
            sum_step(j)

        @pl.loop(lag, CHUNKS)
        def _(j):
            sum_step(j)
            back_step(j - lag, True)

        @pl.loop(CHUNKS - lag, CHUNKS)
        def _(j):
            back_step(j, True)

    @pl.when(place > 0)
    def _():
        for g in range(GROUPS):
            pair(g).wait_recv()

    @pl.when(place == 0)
    def _():
        @pl.loop(0, CHUNKS)
        def _(j):
            back_step(j, False)

    for spot, lag in ((1, 15), (2, 10)):
        @pl.when(place == spot)
        def _():
            relay(lag)

    @pl.when(place == 3)
    def _():
        @pl.loop(0, CHUNKS)
        def _(j):
            finish_step(j)

    @pl.loop(0, CHUNKS)
    def _(j):
        side(j, 1 - core).wait_recv()
        save(j, 1 - core).start()

    for g in range(GROUPS):
        pair(g).wait_send()
        count_copy(g).wait_send()
    for copy in keeps:
        copy.wait()

    @pl.loop(0, CHUNKS)
    def _(j):
        side(j, core).wait_send()
        save(j, 0).wait()
        save(j, 1).wait()

    @pl.when(place < 3)
    def _():
        @pl.loop(0, CHUNKS)
        def _(j):
            onward(j).wait_send()

    @pl.when(place > 0)
    def _():
        @pl.loop(0, CHUNKS)
        def _(j):
            back(j).wait_send()


def row_stage(mesh_shape, tokens, cotangent, w_in, w_out, seg, keep):
    toks, width = tokens.shape
    cols = w_in.shape[1]
    slab = (CHUNKS, 2, toks // PER, cols // 2 // GROUPS)
    dma = pltpu.SemaphoreType.DMA
    args = [
        pltpu.with_memory_space_constraint(x, pltpu.MemorySpace.HBM)
        for x in (tokens, cotangent, w_in, w_out, seg, keep)
    ]
    return pl.pallas_call(
        functools.partial(row_kernel, mesh_shape["batch"]),
        out_shape=(
            jax.ShapeDtypeStruct((2,) + slab, BF16),
            jax.ShapeDtypeStruct((toks, width), BF16),
            jax.ShapeDtypeStruct((toks, width), BF16),
            jax.ShapeDtypeStruct((toks, 256), F32),
        ),
        in_specs=[pl.BlockSpec(memory_space=pltpu.MemorySpace.HBM)] * 6,
        out_specs=(pl.BlockSpec(memory_space=pl.ANY),) * 4,
        scratch_shapes=[
            pltpu.VMEM((toks, width), BF16),
            pltpu.VMEM((toks, width), BF16),
            pltpu.VMEM((width, cols), BF16),
            pltpu.VMEM((cols, width), BF16),
            pltpu.VMEM((1, toks), jnp.int32),
            pltpu.VMEM((1, toks), jnp.int32),
            pltpu.VMEM(slab, BF16),
            pltpu.VMEM(slab, BF16),
            pltpu.VMEM(slab, F32),
            pltpu.VMEM(slab, BF16),
            pltpu.VMEM(slab, BF16),
            pltpu.VMEM((2,) + slab, BF16),
            pltpu.VMEM((toks, width), BF16),
            pltpu.VMEM((toks, width), BF16),
            pltpu.VMEM((toks, 256), F32),
            pltpu.VMEM((SEGS, 128), F32),
            pltpu.VMEM((2, SEGS, 128), F32),
            dma((GROUPS,)), dma((GROUPS,)),
            dma((CHUNKS,)), dma((CHUNKS,)),
            dma((CHUNKS,)), dma((CHUNKS,)),
            dma((CHUNKS,)), dma((CHUNKS,)),
            dma((2,)), dma((2,)),
            dma((2, CHUNKS)), dma((8,)), dma((3,)),
        ],
        compiler_params=pltpu.CompilerParams(
            collective_id=0, has_side_effects=True, vmem_limit_bytes=36 << 20
        ),
        cost_estimate=pl.CostEstimate(
            flops=4 * toks * width * cols, bytes_accessed=40 << 20, transcendentals=0
        ),
        name="row_stage",
    )(*args)


STREAMS = 4


def grad_kernel(
    n_batch, n_x, n_z,
    hid, w_tok, w_cot, w_in, weights,
    g_tok, g_in, g_out,
    grads, y_first, y_rest, part, x_first, x_last, z_send, z_recv, total,
    y_s, y_r, x_s, x_r, z_s, z_r, zg_s, zg_r, xg_s, xg_r, out_sem,
):
    b = lax.axis_index("batch")
    col = lax.axis_index("col")
    xi = col // n_z
    q = col % n_z
    wide = hid.shape[4]
    toks = w_tok.shape[0]
    third = part.shape[2]
    piece = grads.shape[3]
    split = piece // 2
    own_rows = toks // n_x
    own_part = own_rows // STREAMS
    own_split = own_part // 2

    y_next = {"batch": (b + 1) % n_batch}
    y_prev = {"batch": (b + n_batch - 1) % n_batch}
    x_next = {"col": ((xi + 1) % n_x) * n_z + q}
    x_prev = {"col": ((xi + n_x - 1) % n_x) * n_z + q}
    z_one = {"col": xi * n_z + (q + 1) % n_z}
    z_two = {"col": xi * n_z + (q + 2) % n_z}
    y_to = (y_next, y_prev)
    x_to = (x_next, x_prev)
    z_to = (z_one, z_two)

    barrier = pltpu.get_barrier_semaphore()
    for where in y_to + x_to + z_to:
        pl.semaphore_signal(barrier, inc=1, device_id=where, device_id_type=MESH)

    blocks = [(h, g) for h in range(2) for g in range(GROUPS)]

    def hidden(h, g, a):
        return hid[h, g * PER:(g + 1) * PER, a].reshape(toks, wide)

    def place(h, g):
        first = (h * GROUPS + g) * wide
        return slice(first, first + wide)

    def rows_of(ref, owner, start, size):
        first = pl.multiple_of(owner * own_rows + start, size)
        return ref.at[:, pl.ds(first, size), :]

    x_far = (xi + 2) % n_x
    x_near = ((xi + 1) % n_x, (xi + n_x - 1) % n_x)

    def x_sum(u, s, d):
        start = u * own_part
        if s == 0:
            src = rows_of(part, x_far, start + d * own_split, own_split)
            dst = x_first.at[u, d]
        else:
            src = rows_of(part, x_near[d], start, own_part)
            dst = x_last.at[u, d]
        return remote(src, dst, x_s.at[u, s, d], x_r.at[u, s, d], x_to[d])

    def y_owner(s, d):
        shift = 4 - s
        return (b + shift) % n_batch if d == 0 else (b + n_batch - shift) % n_batch

    def y_sum(a, h, s, d):
        src = grads.at[a, h, y_owner(s, d)]
        if s == 0:
            src = src.at[pl.ds(d * split, split), :]
            dst = y_first.at[a, h, d]
        else:
            dst = y_rest.at[a, h, d, s - 1]
        return remote(src, dst, y_s.at[a, h, s, d], y_r.at[a, h, s, d], y_to[d])

    sources = (w_tok, w_cot)

    def products(a, h):
        for g in range(GROUPS):
            block = dot(sources[a][...], hidden(h, g, 1 - a), 0, 0)
            grads[a, h, :, :, g * wide:(g + 1) * wide] = block.reshape(
                n_batch, piece, wide
            ).astype(BF16)

    def y_begin(a, h):
        y_sum(a, h, 0, 0).start()
        y_sum(a, h, 0, 1).start()

    def input_products():
        for i in range(3):
            rows = pl.ds(i * third, third)
            raw = sum(
                dot(hidden(h, g, 1), w_in[rows, place(h, g)], 1, 1) for h, g in blocks
            )
            part[i] = (raw * weights[...]).astype(BF16)

    def x_begin():
        for u in range(STREAMS):
            x_sum(u, 0, 0).start()
            x_sum(u, 0, 1).start()

    def y_onward(a, h, s):
        for d in range(2):
            y_sum(a, h, s - 1, d).wait_recv()
            owner = y_owner(s, d)
            if s == 1:
                lines = pl.ds(d * split, split)
                grads[a, h, owner, lines, :] = (
                    grads[a, h, owner, lines, :].astype(F32)
                    + y_first[a, h, d].astype(F32)
                ).astype(BF16)
            else:
                grads[a, h, owner] = (
                    grads[a, h, owner].astype(F32) + y_rest[a, h, d, s - 2].astype(F32)
                ).astype(BF16)
            y_sum(a, h, s, d).start()

    outs = (g_in, g_out)

    def y_finish(a, h):
        y_sum(a, h, 3, 0).wait_recv()
        y_sum(a, h, 3, 1).wait_recv()
        cols = GROUPS * wide
        outs[a][:, h * cols:(h + 1) * cols] = (
            grads[a, h, b].astype(F32)
            + y_rest[a, h, 0, 2].astype(F32)
            + y_rest[a, h, 1, 2].astype(F32)
        ).astype(BF16)

    def x_onward(u):
        for d in range(2):
            x_sum(u, 0, d).wait_recv()
            first = x_near[d] * own_rows + u * own_part + d * own_split
            lines = pl.ds(pl.multiple_of(first, own_split), own_split)
            part[:, lines, :] = (
                part[:, lines, :].astype(F32) + x_first[u, d].astype(F32)
            ).astype(BF16)
            x_sum(u, 1, d).start()

    def z_sum(u, k):
        target = (q + 1 + k) % n_z
        return remote(
            z_send.at[u, target], z_recv.at[u, k], z_s.at[u, k], z_r.at[u, k], z_to[k]
        )

    def mine(u):
        return pl.ds(pl.multiple_of(xi * own_rows + u * own_part, own_part), own_part)

    def z_scatter(u):
        x_sum(u, 1, 0).wait_recv()
        x_sum(u, 1, 1).wait_recv()
        z_send[u] = (
            part[:, mine(u), :].astype(F32)
            + x_last[u, 0].astype(F32)
            + x_last[u, 1].astype(F32)
        ).astype(BF16)
        z_sum(u, 0).start()
        z_sum(u, 1).start()

    def z_give(u, k):
        spot = total.at[q, mine(u), :]
        return remote(spot, spot, zg_s.at[u, k], zg_r.at[u, k], z_to[k])

    def z_gather(u):
        z_sum(u, 0).wait_recv()
        z_sum(u, 1).wait_recv()
        total[q, mine(u), :] = (
            z_send[u, q].astype(F32)
            + z_recv[u, 0].astype(F32)
            + z_recv[u, 1].astype(F32)
        ).astype(BF16)
        z_give(u, 0).start()
        z_give(u, 1).start()

    def x_give(u, s, d):
        start = u * own_part
        if s == 0:
            spot = rows_of(total, xi, start, own_part)
        else:
            spot = rows_of(total, x_near[1 - d], start + d * own_split, own_split)
        return remote(spot, spot, xg_s.at[u, s, d], xg_r.at[u, s, d], x_to[d])

    def x_gather(u):
        z_give(u, 0).wait_recv()
        z_give(u, 1).wait_recv()
        x_give(u, 0, 0).start()
        x_give(u, 0, 1).start()

    def x_forward(u):
        for d in range(2):
            x_give(u, 0, d).wait_recv()
            x_give(u, 1, d).start()

    def save(i):
        return pltpu.make_async_copy(
            total.at[i], g_tok.at[:, pl.ds(i * third, third)], out_sem.at[i]
        )

    def x_finish(u):
        x_give(u, 1, 0).wait_recv()
        x_give(u, 1, 1).wait_recv()

    products(0, 0)
    input_products()
    pl.semaphore_wait(barrier, 6)
    x_begin()
    y_begin(0, 0)
    products(0, 1)
    y_begin(0, 1)
    products(1, 0)
    products(1, 1)
    y_begin(1, 0)
    x_onward(0)
    y_begin(1, 1)
    x_onward(1)
    y_onward(0, 0, 1)
    x_onward(2)
    y_onward(0, 1, 1)
    x_onward(3)
    y_onward(1, 1, 1)
    z_scatter(1)
    z_scatter(2)
    y_onward(0, 0, 2)
    z_scatter(3)
    y_onward(1, 0, 1)
    z_scatter(0)
    y_onward(1, 1, 2)
    y_onward(0, 1, 2)
    z_gather(1)
    z_gather(2)
    z_gather(3)
    z_gather(0)
    y_onward(1, 0, 2)
    y_onward(1, 1, 3)
    y_onward(0, 0, 3)
    x_gather(2)
    y_onward(0, 1, 3)
    x_gather(1)
    y_onward(1, 0, 3)
    x_gather(0)
    x_gather(3)
    x_forward(1)
    x_forward(0)
    x_forward(2)
    y_finish(0, 0)
    y_finish(1, 1)
    x_forward(3)
    x_finish(0)
    y_finish(0, 1)
    y_finish(1, 0)
    x_finish(3)
    x_finish(2)
    x_finish(1)
    for i in range(3):
        save(i).start()

    for d in range(2):
        for u in range(STREAMS):
            z_sum(u, d).wait_send()
            z_give(u, d).wait_send()
            for s in range(2):
                x_sum(u, s, d).wait_send()
                x_give(u, s, d).wait_send()
        for s in range(4):
            for a in range(2):
                for h in range(2):
                    y_sum(a, h, s, d).wait_send()
    for i in range(3):
        save(i).wait()


def grad_stage(mesh_shape, hid, w_tok, w_cot, w_in, weights):
    n_batch = mesh_shape["batch"]
    n_x, n_z = 4, mesh_shape["col"] // 4
    toks, width = w_tok.shape
    cols = w_in.shape[1]
    third = width // 3
    piece = width // n_batch
    own = toks // n_x // STREAMS
    dma = pltpu.SemaphoreType.DMA
    vmem = pl.BlockSpec(memory_space=pltpu.VMEM)
    return pl.pallas_call(
        functools.partial(grad_kernel, n_batch, n_x, n_z),
        out_shape=(
            jax.ShapeDtypeStruct((toks, width), BF16),
            jax.ShapeDtypeStruct((piece, cols), BF16),
            jax.ShapeDtypeStruct((piece, cols), BF16),
        ),
        in_specs=[vmem] * 5,
        out_specs=(pl.BlockSpec(memory_space=pl.ANY), vmem, vmem),
        scratch_shapes=[
            pltpu.VMEM((2, 2, n_batch, piece, cols // 2), BF16),
            pltpu.VMEM((2, 2, 2, piece // 2, cols // 2), BF16),
            pltpu.VMEM((2, 2, 2, 3, piece, cols // 2), BF16),
            pltpu.VMEM((3, toks, third), BF16),
            pltpu.VMEM((STREAMS, 2, 3, own // 2, third), BF16),
            pltpu.VMEM((STREAMS, 2, 3, own, third), BF16),
            pltpu.VMEM((STREAMS, 3, own, third), BF16),
            pltpu.VMEM((STREAMS, 2, own, third), BF16),
            pltpu.VMEM((3, toks, third), BF16),
            dma((2, 2, 4, 2)), dma((2, 2, 4, 2)),
            dma((STREAMS, 2, 2)), dma((STREAMS, 2, 2)),
            dma((STREAMS, 2)), dma((STREAMS, 2)),
            dma((STREAMS, 2)), dma((STREAMS, 2)),
            dma((STREAMS, 2, 2)), dma((STREAMS, 2, 2)),
            dma((3,)),
        ],
        compiler_params=pltpu.CompilerParams(
            collective_id=1, has_side_effects=True, vmem_limit_bytes=36 << 20
        ),
        cost_estimate=pl.CostEstimate(
            flops=6 * toks * width * cols, bytes_accessed=40 << 20, transcendentals=0
        ),
        name="grad_stage",
    )(hid, w_tok, w_cot, w_in, weights)


def publish_kernel(*refs):
    count = (len(refs) - 1) // 2
    copies = [
        pltpu.make_async_copy(refs[i], refs[count + i], refs[-1].at[i])
        for i in range(count)
    ]
    for copy in copies:
        copy.start()
    for copy in copies:
        copy.wait()


def publish(*arrays):
    anywhere = pl.BlockSpec(memory_space=pl.ANY)
    return pl.pallas_call(
        publish_kernel,
        out_shape=tuple(jax.ShapeDtypeStruct(x.shape, x.dtype) for x in arrays),
        in_specs=[anywhere] * len(arrays),
        out_specs=(anywhere,) * len(arrays),
        scratch_shapes=[pltpu.SemaphoreType.DMA((len(arrays),))],
        compiler_params=pltpu.CompilerParams(vmem_limit_bytes=8 << 20),
        name="publish",
    )(*arrays)


def per_device(mesh_shape, tokens, cotangent, weight_in, weight_out, segment_ids, keep_mask):
    hid, w_tok, w_cot, weights = row_stage(
        mesh_shape, tokens, cotangent, weight_in, weight_out,
        segment_ids[None, :], keep_mask[None, :],
    )
    grad_tokens, grad_in, grad_out = publish(
        *grad_stage(mesh_shape, hid, w_tok, w_cot, weight_in, weights)
    )
    return (grad_tokens, grad_in, grad_out.T)


def solution(mesh):
    return jax.shard_map(
        functools.partial(per_device, dict(mesh.shape)),
        mesh=mesh,
        in_specs=(
            P("batch", "row"),
            P("batch", "row"),
            P("row", "col"),
            P("col", "row"),
            P("batch"),
            P("batch"),
        ),
        out_specs=(P("batch", "row"), P(("row", "batch"), "col"), P("col", ("row", "batch"))),
        check_vma=False,
    )
```

```python
import functools

import jax
import jax.numpy as jnp
from jax import lax
from jax.experimental import pallas as pl
from jax.experimental.pallas import tpu as pltpu
from jax.sharding import PartitionSpec as P

SEGS = 32
IMAGE_MEAN = 128.0
MESH = pl.DeviceIdType.MESH

inv_root_two = 0.7071067811865476
inv_root_tau = 0.3989422804014327

F32 = jnp.float32
BF16 = jnp.bfloat16


def dot(left, right, lc, rc):
    return lax.dot_general(
        left, right, (((lc,), (rc,)), ((), ())), preferred_element_type=F32
    )


def gelu_parts(pre_act):
    normal_cdf = 0.5 * (1.0 + lax.erf(pre_act * inv_root_two))
    slopes = normal_cdf + pre_act * jnp.exp(-0.5 * pre_act * pre_act) * inv_root_tau
    return (pre_act * normal_cdf, slopes)


def remote(src, dst, send, recv, where):
    return pltpu.make_async_remote_copy(
        src_ref=src,
        dst_ref=dst,
        send_sem=send,
        recv_sem=recv,
        device_id=where,
        device_id_type=MESH,
    )


GROUPS = 2
PER = 16
CHUNKS = GROUPS * PER


def row_kernel(
    n_batch,
    tokens_h, cotangent_h, w_in_h, w_out_h, seg_h, keep_h,
    hid_out, w_tok_out, w_cot_out, weight_out,
    tokens, cotangent, w_in, w_out, seg, keep,
    snd, prt, acc, rcv, run, hid,
    w_tok, w_cot, weights, counts, counts_in,
    pair_s, pair_r, sum_s, sum_r, back_s, back_r, side_s, side_r,
    count_s, count_r, out_sem, in_sem, w_sem,
):
    b = lax.axis_index("batch")
    row = lax.axis_index("row")
    core = row % 2
    z = row // 2
    place = core * z + (1 - core) * (3 - z)
    step = 4 * core - 2
    ahead = {"row": (row + step + 8) % 8}
    behind = {"row": (row - step + 8) % 8}
    partner = {"row": row + 1 - 2 * core}
    y_to = ({"batch": (b + 1) % n_batch}, {"batch": (b + n_batch - 1) % n_batch})
    rows, wide = acc.shape[2], acc.shape[3]
    toks, width = tokens.shape
    half = GROUPS * wide

    barrier = pltpu.get_barrier_semaphore()
    for where in (partner, ahead, behind) + y_to:
        pl.semaphore_signal(barrier, inc=1, device_id=where, device_id_type=MESH)

    def columns(which):
        return pl.ds(pl.multiple_of(which * half, half), half)

    other = columns(1 - core)
    mine = columns(core)
    loads = [
        pltpu.make_async_copy(src, dst, in_sem.at[i])
        for i, (src, dst) in enumerate((
            (seg_h, seg),
            (keep_h, keep),
            (tokens_h, tokens),
            (w_in_h.at[:, other], w_in.at[:, other]),
            (cotangent_h, cotangent),
            (w_out_h.at[other, :], w_out.at[other, :]),
            (w_in_h.at[:, mine], w_in.at[:, mine]),
            (w_out_h.at[mine, :], w_out.at[mine, :]),
        ))
    ]
    for load in loads:
        load.start()

    loads[0].wait()
    loads[1].wait()
    labels = lax.broadcasted_iota(jnp.int32, (SEGS, toks), 0)

    def image_marks():
        return jnp.where((labels == seg[...]) & (keep[...] == 1), 1.0, 0.0).astype(F32)

    counts[...] = jnp.broadcast_to(
        jnp.sum(image_marks(), axis=1, keepdims=True), counts.shape
    )

    def count_copy(d):
        return remote(counts, counts_in.at[d], count_s.at[d], count_r.at[d], y_to[d])

    def pair(g):
        part = pl.ds(g * PER, PER)
        return remote(snd.at[part], prt.at[part], pair_s.at[g], pair_r.at[g], partner)

    def products(which, g, into):
        cols = pl.ds(pl.multiple_of(which * half + g * wide, wide), wide)
        part = pl.ds(g * PER, PER)
        fwd = dot(tokens[...], w_in[:, cols], 1, 0)
        into[part, 0] = fwd.reshape(PER, rows, wide).astype(into.dtype)
        bwd = dot(cotangent[...], w_out[cols, :], 1, 1)
        into[part, 1] = bwd.reshape(PER, rows, wide).astype(into.dtype)

    def onward(j):
        return remote(run.at[j], rcv.at[j], sum_s.at[j], sum_r.at[j], ahead)

    def back(j):
        spot = hid.at[core, j]
        return remote(spot, spot, back_s.at[j], back_r.at[j], behind)

    def side(j, which):
        spot = hid.at[which, j]
        return remote(spot, spot, side_s.at[j], side_r.at[j], partner)

    def save(j, which):
        return pltpu.make_async_copy(
            hid.at[which, j], hid_out.at[which, j], out_sem.at[which, j]
        )

    def begin(g):
        @pl.when(place == 0)
        def _():
            pair(g).wait_recv()

            @pl.loop(g * PER, (g + 1) * PER)
            def _(j):
                run[j] = (acc[j] + prt[j].astype(F32)).astype(BF16)
                onward(j).start()

    for load in loads[2:6]:
        load.wait()
    products(1 - core, 0, snd)
    pl.semaphore_wait(barrier, 5)
    pair(0).start()
    count_copy(0).start()
    count_copy(1).start()
    products(1 - core, 1, snd)
    pair(1).start()
    loads[6].wait()
    loads[7].wait()
    products(core, 0, acc)
    begin(0)
    products(core, 1, acc)
    begin(1)

    count_copy(0).wait_recv()
    count_copy(1).wait_recv()
    sizes = counts[...] + counts_in[0] + counts_in[1]
    sizes = jnp.concatenate([sizes, sizes], axis=1)
    per_token = dot(image_marks(), sizes, 0, 0)
    weight = jnp.where(
        per_token > 0.0, jnp.sqrt(IMAGE_MEAN / jnp.maximum(per_token, 1.0)), 0.0
    )
    weights[...] = weight
    span = weight.shape[1]
    for i in range(width // span):
        lanes = pl.ds(i * span, span)
        w_tok[:, lanes] = (tokens[:, lanes].astype(F32) * weight).astype(BF16)
        w_cot[:, lanes] = (cotangent[:, lanes].astype(F32) * weight).astype(BF16)
    keeps = [
        pltpu.make_async_copy(src, dst, w_sem.at[i])
        for i, (src, dst) in enumerate((
            (w_tok, w_tok_out), (w_cot, w_cot_out), (weights, weight_out),
        ))
    ]
    for copy in keeps:
        copy.start()

    def sum_step(j):
        own = acc[j] + prt[j].astype(F32)
        onward(j).wait_recv()
        run[j] = (own + rcv[j].astype(F32)).astype(BF16)
        onward(j).start()

    def finish_step(j):
        onward(j).wait_recv()
        pre = acc[j, 0] + prt[j, 0].astype(F32) + rcv[j, 0].astype(F32)
        grad = acc[j, 1] + prt[j, 1].astype(F32) + rcv[j, 1].astype(F32)
        act, slopes = gelu_parts(pre)
        hid[core, j, 0] = act.astype(BF16)
        hid[core, j, 1] = (grad * slopes).astype(BF16)
        back(j).start()
        side(j, core).start()
        save(j, core).start()

    def back_step(j, further):
        back(j).wait_recv()
        if further:
            back(j).start()
        side(j, core).start()
        save(j, core).start()

    def relay(lag):
        @pl.loop(0, lag)
        def _(j):
            sum_step(j)

        @pl.loop(lag, CHUNKS)
        def _(j):
            sum_step(j)
            back_step(j - lag, True)

        @pl.loop(CHUNKS - lag, CHUNKS)
        def _(j):
            back_step(j, True)

    @pl.when(place > 0)
    def _():
        for g in range(GROUPS):
            pair(g).wait_recv()

    @pl.when(place == 0)
    def _():
        @pl.loop(0, CHUNKS)
        def _(j):
            back_step(j, False)

    for spot, lag in ((1, 31), (2, 19)):
        @pl.when(place == spot)
        def _():
            relay(lag)

    @pl.when(place == 3)
    def _():
        @pl.loop(0, CHUNKS)
        def _(j):
            finish_step(j)

    @pl.loop(0, CHUNKS)
    def _(j):
        side(j, 1 - core).wait_recv()
        save(j, 1 - core).start()

    for g in range(GROUPS):
        pair(g).wait_send()
        count_copy(g).wait_send()
    for copy in keeps:
        copy.wait()

    @pl.loop(0, CHUNKS)
    def _(j):
        side(j, core).wait_send()
        save(j, 0).wait()
        save(j, 1).wait()

    @pl.when(place < 3)
    def _():
        @pl.loop(0, CHUNKS)
        def _(j):
            onward(j).wait_send()

    @pl.when(place > 0)
    def _():
        @pl.loop(0, CHUNKS)
        def _(j):
            back(j).wait_send()


def row_stage(mesh_shape, tokens, cotangent, w_in, w_out, seg, keep):
    toks, width = tokens.shape
    cols = w_in.shape[1]
    slab = (CHUNKS, 2, toks // PER, cols // 2 // GROUPS)
    dma = pltpu.SemaphoreType.DMA
    args = [
        pltpu.with_memory_space_constraint(x, pltpu.MemorySpace.HBM)
        for x in (tokens, cotangent, w_in, w_out, seg, keep)
    ]
    return pl.pallas_call(
        functools.partial(row_kernel, mesh_shape["batch"]),
        out_shape=(
            jax.ShapeDtypeStruct((2,) + slab, BF16),
            jax.ShapeDtypeStruct((toks, width), BF16),
            jax.ShapeDtypeStruct((toks, width), BF16),
            jax.ShapeDtypeStruct((toks, 256), F32),
        ),
        in_specs=[pl.BlockSpec(memory_space=pltpu.MemorySpace.HBM)] * 6,
        out_specs=(pl.BlockSpec(memory_space=pl.ANY),) * 4,
        scratch_shapes=[
            pltpu.VMEM((toks, width), BF16),
            pltpu.VMEM((toks, width), BF16),
            pltpu.VMEM((width, cols), BF16),
            pltpu.VMEM((cols, width), BF16),
            pltpu.VMEM((1, toks), jnp.int32),
            pltpu.VMEM((1, toks), jnp.int32),
            pltpu.VMEM(slab, BF16),
            pltpu.VMEM(slab, BF16),
            pltpu.VMEM(slab, F32),
            pltpu.VMEM(slab, BF16),
            pltpu.VMEM(slab, BF16),
            pltpu.VMEM((2,) + slab, BF16),
            pltpu.VMEM((toks, width), BF16),
            pltpu.VMEM((toks, width), BF16),
            pltpu.VMEM((toks, 256), F32),
            pltpu.VMEM((SEGS, 128), F32),
            pltpu.VMEM((2, SEGS, 128), F32),
            dma((GROUPS,)), dma((GROUPS,)),
            dma((CHUNKS,)), dma((CHUNKS,)),
            dma((CHUNKS,)), dma((CHUNKS,)),
            dma((CHUNKS,)), dma((CHUNKS,)),
            dma((2,)), dma((2,)),
            dma((2, CHUNKS)), dma((8,)), dma((3,)),
        ],
        compiler_params=pltpu.CompilerParams(
            collective_id=0, has_side_effects=True, vmem_limit_bytes=36 << 20
        ),
        cost_estimate=pl.CostEstimate(
            flops=4 * toks * width * cols, bytes_accessed=40 << 20, transcendentals=0
        ),
        name="row_stage",
    )(*args)


STREAMS = 4


def grad_kernel(
    n_batch, n_x, n_z,
    hid, w_tok, w_cot, w_in, weights,
    g_tok, g_in, g_out,
    grads, y_first, y_rest, part, x_first, x_last, z_send, z_recv, total,
    y_s, y_r, x_s, x_r, z_s, z_r, zg_s, zg_r, xg_s, xg_r, out_sem,
):
    b = lax.axis_index("batch")
    col = lax.axis_index("col")
    xi = col // n_z
    q = col % n_z
    wide = hid.shape[4]
    toks = w_tok.shape[0]
    third = part.shape[2]
    piece = grads.shape[3]
    split = piece // 2
    own_rows = toks // n_x
    own_part = own_rows // STREAMS
    own_split = own_part // 2

    y_next = {"batch": (b + 1) % n_batch}
    y_prev = {"batch": (b + n_batch - 1) % n_batch}
    x_next = {"col": ((xi + 1) % n_x) * n_z + q}
    x_prev = {"col": ((xi + n_x - 1) % n_x) * n_z + q}
    z_one = {"col": xi * n_z + (q + 1) % n_z}
    z_two = {"col": xi * n_z + (q + 2) % n_z}
    y_to = (y_next, y_prev)
    x_to = (x_next, x_prev)
    z_to = (z_one, z_two)

    barrier = pltpu.get_barrier_semaphore()
    for where in y_to + x_to + z_to:
        pl.semaphore_signal(barrier, inc=1, device_id=where, device_id_type=MESH)

    blocks = [(h, g) for h in range(2) for g in range(GROUPS)]

    def hidden(h, g, a):
        return hid[h, g * PER:(g + 1) * PER, a].reshape(toks, wide)

    def place(h, g):
        first = (h * GROUPS + g) * wide
        return slice(first, first + wide)

    def rows_of(ref, owner, start, size):
        first = pl.multiple_of(owner * own_rows + start, size)
        return ref.at[:, pl.ds(first, size), :]

    x_far = (xi + 2) % n_x
    x_near = ((xi + 1) % n_x, (xi + n_x - 1) % n_x)

    def x_sum(u, s, d):
        start = u * own_part
        if s == 0:
            src = rows_of(part, x_far, start + d * own_split, own_split)
            dst = x_first.at[u, d]
        else:
            src = rows_of(part, x_near[d], start, own_part)
            dst = x_last.at[u, d]
        return remote(src, dst, x_s.at[u, s, d], x_r.at[u, s, d], x_to[d])

    def y_owner(s, d):
        shift = 4 - s
        return (b + shift) % n_batch if d == 0 else (b + n_batch - shift) % n_batch

    def y_sum(a, h, s, d):
        src = grads.at[a, h, y_owner(s, d)]
        if s == 0:
            src = src.at[pl.ds(d * split, split), :]
            dst = y_first.at[a, h, d]
        else:
            dst = y_rest.at[a, h, d, s - 1]
        return remote(src, dst, y_s.at[a, h, s, d], y_r.at[a, h, s, d], y_to[d])

    sources = (w_tok, w_cot)

    def products(a, h):
        for g in range(GROUPS):
            block = dot(sources[a][...], hidden(h, g, 1 - a), 0, 0)
            grads[a, h, :, :, g * wide:(g + 1) * wide] = block.reshape(
                n_batch, piece, wide
            ).astype(BF16)

    def y_begin(a, h):
        y_sum(a, h, 0, 0).start()
        y_sum(a, h, 0, 1).start()

    def input_products():
        for i in range(3):
            rows = pl.ds(i * third, third)
            raw = sum(
                dot(hidden(h, g, 1), w_in[rows, place(h, g)], 1, 1) for h, g in blocks
            )
            part[i] = (raw * weights[...]).astype(BF16)

    def x_begin():
        for u in range(STREAMS):
            x_sum(u, 0, 0).start()
            x_sum(u, 0, 1).start()

    def y_onward(a, h, s):
        for d in range(2):
            y_sum(a, h, s - 1, d).wait_recv()
            owner = y_owner(s, d)
            if s == 1:
                lines = pl.ds(d * split, split)
                grads[a, h, owner, lines, :] = (
                    grads[a, h, owner, lines, :].astype(F32)
                    + y_first[a, h, d].astype(F32)
                ).astype(BF16)
            else:
                grads[a, h, owner] = (
                    grads[a, h, owner].astype(F32) + y_rest[a, h, d, s - 2].astype(F32)
                ).astype(BF16)
            y_sum(a, h, s, d).start()

    outs = (g_in, g_out)

    def y_finish(a, h):
        y_sum(a, h, 3, 0).wait_recv()
        y_sum(a, h, 3, 1).wait_recv()
        cols = GROUPS * wide
        outs[a][:, h * cols:(h + 1) * cols] = (
            grads[a, h, b].astype(F32)
            + y_rest[a, h, 0, 2].astype(F32)
            + y_rest[a, h, 1, 2].astype(F32)
        ).astype(BF16)

    def x_onward(u):
        for d in range(2):
            x_sum(u, 0, d).wait_recv()
            first = x_near[d] * own_rows + u * own_part + d * own_split
            lines = pl.ds(pl.multiple_of(first, own_split), own_split)
            part[:, lines, :] = (
                part[:, lines, :].astype(F32) + x_first[u, d].astype(F32)
            ).astype(BF16)
            x_sum(u, 1, d).start()

    def z_sum(u, k):
        target = (q + 1 + k) % n_z
        return remote(
            z_send.at[u, target], z_recv.at[u, k], z_s.at[u, k], z_r.at[u, k], z_to[k]
        )

    def mine(u):
        return pl.ds(pl.multiple_of(xi * own_rows + u * own_part, own_part), own_part)

    def z_scatter(u):
        x_sum(u, 1, 0).wait_recv()
        x_sum(u, 1, 1).wait_recv()
        z_send[u] = (
            part[:, mine(u), :].astype(F32)
            + x_last[u, 0].astype(F32)
            + x_last[u, 1].astype(F32)
        ).astype(BF16)
        z_sum(u, 0).start()
        z_sum(u, 1).start()

    def z_give(u, k):
        spot = total.at[q, mine(u), :]
        return remote(spot, spot, zg_s.at[u, k], zg_r.at[u, k], z_to[k])

    def z_gather(u):
        z_sum(u, 0).wait_recv()
        z_sum(u, 1).wait_recv()
        total[q, mine(u), :] = (
            z_send[u, q].astype(F32)
            + z_recv[u, 0].astype(F32)
            + z_recv[u, 1].astype(F32)
        ).astype(BF16)
        z_give(u, 0).start()
        z_give(u, 1).start()

    def x_give(u, s, d):
        start = u * own_part
        if s == 0:
            spot = rows_of(total, xi, start, own_part)
        else:
            spot = rows_of(total, x_near[1 - d], start + d * own_split, own_split)
        return remote(spot, spot, xg_s.at[u, s, d], xg_r.at[u, s, d], x_to[d])

    def x_gather(u):
        z_give(u, 0).wait_recv()
        z_give(u, 1).wait_recv()
        x_give(u, 0, 0).start()
        x_give(u, 0, 1).start()

    def x_forward(u):
        for d in range(2):
            x_give(u, 0, d).wait_recv()
            x_give(u, 1, d).start()

    def save(i):
        return pltpu.make_async_copy(
            total.at[i], g_tok.at[:, pl.ds(i * third, third)], out_sem.at[i]
        )

    def x_finish(u):
        x_give(u, 1, 0).wait_recv()
        x_give(u, 1, 1).wait_recv()

    products(0, 0)
    input_products()
    pl.semaphore_wait(barrier, 6)
    x_begin()
    y_begin(0, 0)
    products(0, 1)
    y_begin(0, 1)
    products(1, 0)
    products(1, 1)
    y_begin(1, 0)
    x_onward(0)
    y_begin(1, 1)
    x_onward(1)
    y_onward(0, 0, 1)
    x_onward(2)
    y_onward(0, 1, 1)
    x_onward(3)
    y_onward(1, 1, 1)
    z_scatter(1)
    z_scatter(2)
    y_onward(0, 0, 2)
    z_scatter(3)
    y_onward(1, 0, 1)
    z_scatter(0)
    y_onward(1, 1, 2)
    y_onward(0, 1, 2)
    z_gather(1)
    z_gather(2)
    z_gather(3)
    z_gather(0)
    y_onward(1, 0, 2)
    y_onward(1, 1, 3)
    y_onward(0, 0, 3)
    x_gather(2)
    y_onward(0, 1, 3)
    x_gather(1)
    y_onward(1, 0, 3)
    x_gather(0)
    x_gather(3)
    x_forward(1)
    x_forward(0)
    x_forward(2)
    y_finish(0, 0)
    y_finish(1, 1)
    x_forward(3)
    x_finish(0)
    y_finish(0, 1)
    y_finish(1, 0)
    x_finish(3)
    x_finish(2)
    x_finish(1)
    for i in range(3):
        save(i).start()

    for d in range(2):
        for u in range(STREAMS):
            z_sum(u, d).wait_send()
            z_give(u, d).wait_send()
            for s in range(2):
                x_sum(u, s, d).wait_send()
                x_give(u, s, d).wait_send()
        for s in range(4):
            for a in range(2):
                for h in range(2):
                    y_sum(a, h, s, d).wait_send()
    for i in range(3):
        save(i).wait()


def grad_stage(mesh_shape, hid, w_tok, w_cot, w_in, weights):
    n_batch = mesh_shape["batch"]
    n_x, n_z = 4, mesh_shape["col"] // 4
    toks, width = w_tok.shape
    cols = w_in.shape[1]
    third = width // 3
    piece = width // n_batch
    own = toks // n_x // STREAMS
    dma = pltpu.SemaphoreType.DMA
    vmem = pl.BlockSpec(memory_space=pltpu.VMEM)
    return pl.pallas_call(
        functools.partial(grad_kernel, n_batch, n_x, n_z),
        out_shape=(
            jax.ShapeDtypeStruct((toks, width), BF16),
            jax.ShapeDtypeStruct((piece, cols), BF16),
            jax.ShapeDtypeStruct((piece, cols), BF16),
        ),
        in_specs=[vmem] * 5,
        out_specs=(pl.BlockSpec(memory_space=pl.ANY), vmem, vmem),
        scratch_shapes=[
            pltpu.VMEM((2, 2, n_batch, piece, cols // 2), BF16),
            pltpu.VMEM((2, 2, 2, piece // 2, cols // 2), BF16),
            pltpu.VMEM((2, 2, 2, 3, piece, cols // 2), BF16),
            pltpu.VMEM((3, toks, third), BF16),
            pltpu.VMEM((STREAMS, 2, 3, own // 2, third), BF16),
            pltpu.VMEM((STREAMS, 2, 3, own, third), BF16),
            pltpu.VMEM((STREAMS, 3, own, third), BF16),
            pltpu.VMEM((STREAMS, 2, own, third), BF16),
            pltpu.VMEM((3, toks, third), BF16),
            dma((2, 2, 4, 2)), dma((2, 2, 4, 2)),
            dma((STREAMS, 2, 2)), dma((STREAMS, 2, 2)),
            dma((STREAMS, 2)), dma((STREAMS, 2)),
            dma((STREAMS, 2)), dma((STREAMS, 2)),
            dma((STREAMS, 2, 2)), dma((STREAMS, 2, 2)),
            dma((3,)),
        ],
        compiler_params=pltpu.CompilerParams(
            collective_id=1, has_side_effects=True, vmem_limit_bytes=36 << 20
        ),
        cost_estimate=pl.CostEstimate(
            flops=6 * toks * width * cols, bytes_accessed=40 << 20, transcendentals=0
        ),
        name="grad_stage",
    )(hid, w_tok, w_cot, w_in, weights)


def publish_kernel(*refs):
    count = (len(refs) - 1) // 2
    copies = [
        pltpu.make_async_copy(refs[i], refs[count + i], refs[-1].at[i])
        for i in range(count)
    ]
    for copy in copies:
        copy.start()
    for copy in copies:
        copy.wait()


def publish(*arrays):
    anywhere = pl.BlockSpec(memory_space=pl.ANY)
    return pl.pallas_call(
        publish_kernel,
        out_shape=tuple(jax.ShapeDtypeStruct(x.shape, x.dtype) for x in arrays),
        in_specs=[anywhere] * len(arrays),
        out_specs=(anywhere,) * len(arrays),
        scratch_shapes=[pltpu.SemaphoreType.DMA((len(arrays),))],
        compiler_params=pltpu.CompilerParams(vmem_limit_bytes=8 << 20),
        name="publish",
    )(*arrays)


def per_device(mesh_shape, tokens, cotangent, weight_in, weight_out, segment_ids, keep_mask):
    hid, w_tok, w_cot, weights = row_stage(
        mesh_shape, tokens, cotangent, weight_in, weight_out,
        segment_ids[None, :], keep_mask[None, :],
    )
    grad_tokens, grad_in, grad_out = publish(
        *grad_stage(mesh_shape, hid, w_tok, w_cot, weight_in, weights)
    )
    return (grad_tokens, grad_in, grad_out.T)


def solution(mesh):
    return jax.shard_map(
        functools.partial(per_device, dict(mesh.shape)),
        mesh=mesh,
        in_specs=(
            P("batch", "row"),
            P("batch", "row"),
            P("row", "col"),
            P("col", "row"),
            P("batch"),
            P("batch"),
        ),
        out_specs=(P("batch", "row"), P(("row", "batch"), "col"), P("col", ("row", "batch"))),
        check_vma=False,
    )
```
